256 devices in a mesh: angle: 8 (over z), strip: 32 (over y, x, core).
Axes of the slice: x: 4, y: 4, z: 8, core: 2. Of those that a mesh axis runs over, the one named last changes fastest.
Arguments:
- object_field: float32 [2, 8, 4096, 1024], P(None, 'angle', 'strip'), may hold values from -5 to 5
- amplitudes: bfloat16 [8, 128, 256, 256], P('angle', 'strip'), may hold values from 0.25 to 4
- scan_offsets: int32 [8, 128, 2], P('angle', 'strip'), may hold values from 0 to 768, as said below
- probe_field: float32 [2, 256, 256], replicated, may hold values from -5 to 5
- tilt_angles: float32 [8], replicated, may hold values from -3.140625 to 3.140625
Outputs:
- object_grad: float32 [2, 8, 4096, 1024], P(None, 'angle', 'strip')
- probe_grad: float32 [2, 256, 256], replicated
- volume_grad: float32 [32, 8, 16, 16384], P('strip', 'angle')
The draws below stay inside these ranges and needn't reach their ends.
Inputs may be any that keep to these rules, and one draw needn't show every extreme that they name: `scan_offsets`: row offsets lie in 0 to 0 and column offsets in 0 to 768. In every strip's block of 4 frames, the first frame has row offset 0 and column offset 768, the second row offset 0 and column offset 0, the third column offset 768 // 2.
All inputs are finite; a program needn't handle non-finite values.
Results may differ from the reference program's by a relative error of at most 0.0079.
The reference program's roundings to bfloat16 on the way count: a program that leaves them out, or rounds other values in their place, can miss the bound.
Values may be sent and summed in bfloat16 or wider, within the bound.
A program may use at most 64 MiB of HBM per device.

```python
import math
import jax
import jax.numpy as jnp
from jax import lax

W = 1024
FRAME = 256
HALO = 64
SR = 128
FRAMES = 4
NG = 128
CELLS = 16384
ANGLES = 8
STRIPS = 32
Z = 4096
FRAMES_ALL = 128
SLICES_DEV = 16
ROWSPAN = 0
COLSPAN = 768


def draw_scan_offsets(key, part):
    key_rows, key_cols = jax.random.split(jax.random.fold_in(key, 17))
    row_offsets = jax.random.randint(key_rows, (ANGLES, STRIPS, FRAMES), 0, ROWSPAN + 1, dtype=jnp.int32)
    col_offsets = jax.random.randint(key_cols, (ANGLES, STRIPS, FRAMES), 0, COLSPAN + 1, dtype=jnp.int32)
    row_offsets = row_offsets.at[:, :, 0].set(0).at[:, :, 1].set(ROWSPAN)
    col_offsets = col_offsets.at[:, :, 0].set(COLSPAN).at[:, :, 1].set(0).at[:, :, 2].set(COLSPAN // 2)
    stacked = jnp.stack([row_offsets, col_offsets], -1)
    return stacked.reshape(ANGLES, STRIPS * FRAMES, 2).astype(jnp.int32)


def level_of(own_key, extent, cuts, low, largest):
    gain, own = 1.0, jax.random.fold_in(own_key, 6)
    for axis_at, blocks in cuts:
        heights = jnp.exp(jax.random.uniform(jax.random.fold_in(own, axis_at), (blocks,), jnp.float32, low / len(cuts), largest / len(cuts)))
        gain = gain * jnp.repeat(heights, extent[axis_at] // blocks).reshape([-1 if axis == axis_at else 1 for axis in range(len(extent))])
    return gain


def gaussian(stream_key, extent, width, reach, pieces=(), kind=jnp.bfloat16):
    gain = level_of(stream_key, extent, pieces, -0.22, 0.18) if pieces else 1.0
    array = jax.random.normal(stream_key, extent, jnp.float32) * width * gain
    return jnp.minimum(jnp.maximum(array, -reach), reach).astype(kind)


def setup_inputs(seed: int = 0) -> dict:
    key_list = jax.random.split(jax.random.key(seed), 6)
    return {
        "object_field": gaussian(key_list[0], (2, ANGLES, Z, W), 0.7, 5.0, ((1, 8), (2, 32)), jnp.float32),
        "amplitudes": jnp.clip(jnp.exp(math.log(4.0) - 2.7725887 * jax.random.uniform(key_list[1], (ANGLES, FRAMES_ALL, FRAME, FRAME), jnp.float32) ** level_of(key_list[1], (ANGLES, FRAMES_ALL, FRAME, FRAME), ((0, 8), (1, 32)), -0.2, 0.2)), 0.25, 4.0).astype(jnp.bfloat16),
        "scan_offsets": draw_scan_offsets(jax.random.fold_in(key_list[5], 71), 0),
        "probe_field": gaussian(key_list[3], (2, FRAME, FRAME), 0.7, 5.0, (), jnp.float32),
        "tilt_angles": jnp.clip(jax.random.uniform(key_list[4], (ANGLES,), jnp.float32, -3.140625, 3.140625), -3.140625, 3.140625),
    }


def dft_tables(size_n):
    indices = jnp.arange(size_n, dtype=jnp.int32)
    product = indices[:, None] * indices[None, :] % size_n
    phase_arg = 2.0 * math.pi / size_n * product.astype(jnp.float32)
    norm_scale = 1.0 / math.sqrt(size_n)
    cos_tab = jnp.cos(phase_arg) * norm_scale
    sin_tab = jnp.sin(phase_arg) * norm_scale
    left_fwd = jnp.stack([jnp.stack([cos_tab, sin_tab]), jnp.stack([-sin_tab, cos_tab])]).astype(jnp.bfloat16)
    right_fwd = jnp.stack([jnp.stack([cos_tab, -sin_tab]), jnp.stack([sin_tab, cos_tab])]).astype(jnp.bfloat16)
    return (left_fwd, right_fwd)

def frame_grads(patches, probe_field, amp_block, left_fwd, right_fwd):
    probe_re, probe_im = (probe_field[0], probe_field[1])
    patch_re, patch_im = (patches[:, 0], patches[:, 1])
    exit_wave = jnp.stack([probe_re * patch_re - probe_im * patch_im, probe_re * patch_im + probe_im * patch_re], 1).astype(jnp.bfloat16)
    half = jnp.einsum('abik,fbkj->faij', left_fwd.astype(jnp.float32), exit_wave.astype(jnp.float32)).astype(jnp.bfloat16)
    wave = jnp.einsum('fbik,bakj->faij', half.astype(jnp.float32), right_fwd.astype(jnp.float32))
    magnitude_sq = wave[:, 0] * wave[:, 0] + wave[:, 1] * wave[:, 1]
    factor = 1.0 - amp_block.astype(jnp.float32) / jnp.sqrt(magnitude_sq + 1.0)
    misfit = (wave * factor[:, None]).astype(jnp.bfloat16)
    back = jnp.einsum('abik,fbkj->faij', right_fwd.astype(jnp.float32), misfit.astype(jnp.float32)).astype(jnp.bfloat16)
    exit_grad = jnp.einsum('fbik,bakj->faij', back.astype(jnp.float32), left_fwd.astype(jnp.float32))
    grad_re, grad_im = (exit_grad[:, 0], exit_grad[:, 1])
    object_terms = jnp.stack([probe_re * grad_re + probe_im * grad_im, probe_re * grad_im - probe_im * grad_re], 1)
    probe_terms = jnp.stack([lax.optimization_barrier(jnp.sum(patch_re * grad_re + patch_im * grad_im, 0)), lax.optimization_barrier(jnp.sum(patch_re * grad_im - patch_im * grad_re, 0))])
    return (object_terms, probe_terms)

def slice_project(rows, theta, side_cells, width_cols):
    cell = jnp.arange(side_cells * side_cells, dtype=jnp.int32)
    center = (side_cells - 1) / 2.0
    xpos = (cell // side_cells).astype(jnp.float32) - center
    ypos = (cell % side_cells).astype(jnp.float32) - center
    upos = (width_cols - 1) / 2.0 + 2.0 * (xpos * jnp.cos(theta) + ypos * jnp.sin(theta))
    lower = jnp.clip(jnp.floor(upos), 0.0, width_cols - 2.0)
    frac = upos - lower
    lower_idx = lower.astype(jnp.int32)
    left = jnp.take(rows, lower_idx, axis=1).astype(jnp.float32)
    right = jnp.take(rows, lower_idx + 1, axis=1).astype(jnp.float32)
    return left * (1.0 - frac) + right * frac

def reference(object_field, amplitudes, scan_offsets, probe_field, tilt_angles):
    left_fwd, right_fwd = dft_tables(FRAME)
    padded = jnp.pad(object_field, ((0, 0), (0, 0), (HALO, HALO), (0, 0)))
    ext_rows = SR + 2 * HALO

    def strip_work(flat_idx):
        angle_idx = (flat_idx // STRIPS).astype(jnp.int32)
        strip_idx = (flat_idx % STRIPS).astype(jnp.int32)
        zero_idx = jnp.int32(0)
        extended = lax.dynamic_slice(padded, (zero_idx, angle_idx, (strip_idx * SR).astype(jnp.int32), zero_idx), (2, 1, ext_rows, W))[:, 0]
        offsets = lax.dynamic_slice(scan_offsets, (angle_idx, (strip_idx * FRAMES).astype(jnp.int32), zero_idx), (1, FRAMES, 2))[0]
        amp_block = lax.dynamic_slice(amplitudes, (angle_idx, (strip_idx * FRAMES).astype(jnp.int32), zero_idx, zero_idx), (1, FRAMES, FRAME, FRAME))[0]

        def take_patch(offset_pair):
            return lax.dynamic_slice(extended, (zero_idx, offset_pair[0].astype(jnp.int32), offset_pair[1].astype(jnp.int32)), (2, FRAME, FRAME))
        patches = jax.vmap(take_patch)(offsets)
        object_terms, probe_terms = frame_grads(patches, probe_field, amp_block, left_fwd, right_fwd)

        def add_frame(frame_idx, accum):
            row_at = offsets[frame_idx, 0].astype(jnp.int32)
            col_at = offsets[frame_idx, 1].astype(jnp.int32)
            current = lax.dynamic_slice(accum, (zero_idx, row_at, col_at), (2, FRAME, FRAME))
            return lax.dynamic_update_slice(accum, current + object_terms[frame_idx], (zero_idx, row_at, col_at))
        ext_grad = lax.fori_loop(0, FRAMES, add_frame, jnp.zeros((2, ext_rows, W), jnp.float32))
        return (ext_grad, probe_terms)
    ext_all, probe_all = lax.map(strip_work, jnp.arange(ANGLES * STRIPS, dtype=jnp.int32))
    ext_all = ext_all.reshape(ANGLES, STRIPS, 2, ext_rows, W)
    core = ext_all[:, :, :, HALO:HALO + SR]
    from_above = jnp.pad(ext_all[:, 1:, :, :HALO], ((0, 0), (0, 1), (0, 0), (0, 0), (0, 0)))
    from_below = jnp.pad(ext_all[:, :-1, :, SR + HALO:], ((0, 0), (1, 0), (0, 0), (0, 0), (0, 0)))
    core = core.at[:, :, :, SR - HALO:].add(from_above)
    core = core.at[:, :, :, :HALO].add(from_below)
    object_grad = core.transpose(2, 0, 1, 3, 4).reshape(2, ANGLES, Z, W)
    probe_grad = lax.optimization_barrier(jnp.sum(probe_all, 0)) * (1.0 / math.sqrt(ANGLES * STRIPS * FRAMES))
    phase = (object_field[0] * object_grad[1] - object_field[1] * object_grad[0]).astype(jnp.bfloat16)

    def slab_work(block_idx):
        zero_idx = jnp.int32(0)

        def add_angle(angle_idx, total_sum):
            angle_at = jnp.asarray(angle_idx).astype(jnp.int32)
            rows = lax.dynamic_slice(phase, (angle_at, (block_idx * SLICES_DEV).astype(jnp.int32), zero_idx), (1, SLICES_DEV, W))[0]
            return total_sum + slice_project(rows, tilt_angles[angle_at], NG, W)
        return lax.fori_loop(0, ANGLES, add_angle, jnp.zeros((SLICES_DEV, CELLS), jnp.float32))
    volume = lax.map(slab_work, jnp.arange(Z // SLICES_DEV, dtype=jnp.int32))
    volume_grad = volume.reshape(STRIPS, ANGLES, SLICES_DEV, CELLS)
    return (object_grad, probe_grad, volume_grad)
```

```python
import math

import jax
import jax.numpy as jnp
import numpy as np
from jax import lax
from jax.experimental import pallas as pl
from jax.experimental.pallas import tpu as pltpu
from jax.sharding import PartitionSpec as P

FRAME = 256
HALO = 64
NG = 128
LANES = 128
MESH = pl.DeviceIdType.MESH
F32 = jnp.float32
BF16 = jnp.bfloat16
FIXED_COLS = (768, 0, 384)
WINDOW = (256, 768)


def dft_blocks():
    index = np.arange(FRAME)
    angle = 2.0 * np.pi / FRAME * ((index[:, None] * index[None, :]) % FRAME)
    cos_tab = np.cos(angle) / math.sqrt(FRAME)
    sin_tab = np.sin(angle) / math.sqrt(FRAME)
    fwd = np.block([[cos_tab, sin_tab], [-sin_tab, cos_tab]])
    inv = np.block([[cos_tab, -sin_tab], [sin_tab, cos_tab]])
    return jnp.asarray(fwd, BF16), jnp.asarray(inv, BF16)


def kernel(
    n_angle, n_strip, scale,
    cols, trig, obj_hbm, amp_hbm, probe_hbm, fwd_hbm, inv_hbm,
    og_hbm, pg_hbm, vol_hbm,
    ext, probe, amp, fwd, inv,
    halo_out, halo_in, place_t, place_m, moved3, patch3, xbuf, ybuf, wbuf, mbuf, zbuf, gbuf,
    grad_out, grad_in, core, phase, ph_all,
    pterm, rs_in, ar_in, ag_in, pg_out,
    lower_t, frac_t, lhs, vol,
    load_sem, store_sem, halo_s, halo_r, grad_s, grad_r, a2a_s, a2a_r,
    rs_s, rs_r, ar_s, ar_r, ag_s, ag_r,
):
    width = ext.shape[2]
    me_a = lax.axis_index("angle")
    me_s = lax.axis_index("strip")
    above = lax.rem(me_s + n_strip - 1, n_strip)
    below = lax.rem(me_s + 1, n_strip)

    loads = [
        pltpu.make_async_copy(obj_hbm, ext.at[:, pl.ds(HALO, 128), :], load_sem.at[0]),
        pltpu.make_async_copy(probe_hbm, probe, load_sem.at[1]),
        pltpu.make_async_copy(inv_hbm, inv, load_sem.at[2]),
        pltpu.make_async_copy(fwd_hbm, fwd, load_sem.at[3]),
        pltpu.make_async_copy(amp_hbm, amp, load_sem.at[4]),
    ]
    for load in loads:
        load.start()

    barrier = pltpu.get_barrier_semaphore()

    @pl.loop(1, n_strip)
    def _(d):
        pl.semaphore_signal(
            barrier, inc=1, device_id={"strip": lax.rem(me_s + d, n_strip)}, device_id_type=MESH
        )

    @pl.loop(1, n_angle)
    def _(d):
        pl.semaphore_signal(
            barrier, inc=1, device_id={"angle": lax.rem(me_a + d, n_angle)}, device_id_type=MESH
        )

    loads[0].wait()
    for side, first in ((0, HALO), (1, 2 * HALO)):

        @pl.loop(0, 4)
        def _(step):
            rows = pl.multiple_of(step * 16, 16)
            for part in range(2):
                halo_out[side, part, pl.ds(rows, 16), :] = ext[
                    part, pl.ds(first + rows, 16), :
                ].astype(BF16)

    pl.semaphore_wait(barrier, n_strip - 1 + n_angle - 1)

    def remote(src, dst, send, recv, **where):
        return pltpu.make_async_remote_copy(
            src_ref=src, dst_ref=dst, send_sem=send, recv_sem=recv,
            device_id=where, device_id_type=MESH,
        )

    halo_copies = [
        remote(halo_out.at[1], halo_in.at[0], halo_s.at[0], halo_r.at[0], strip=below),
        remote(halo_out.at[0], halo_in.at[1], halo_s.at[1], halo_r.at[1], strip=above),
    ]
    for copy in halo_copies:
        copy.start()

    col = cols[0].astype(F32)
    for b in range(width // LANES):
        at = lax.broadcasted_iota(jnp.int32, (LANES, FRAME), 0) + b * LANES
        of = lax.broadcasted_iota(jnp.int32, (LANES, FRAME), 1)
        place_t[b * LANES : (b + 1) * LANES, :] = ((at - of).astype(F32) == col).astype(F32).astype(BF16)
        at = lax.broadcasted_iota(jnp.int32, (FRAME, LANES), 1) + b * LANES
        of = lax.broadcasted_iota(jnp.int32, (FRAME, LANES), 0)
        place_m[:, b * LANES : (b + 1) * LANES] = ((at - of).astype(F32) == col).astype(F32).astype(BF16)

    def split(value):
        high = value.astype(BF16)
        return jnp.concatenate([high, (value - high.astype(F32)).astype(BF16)], axis=0)

    def joined(product):
        rows = product.shape[0] // 2
        return product[:rows] + product[rows:]

    def exit_chunk(chunk):
        rows = pl.ds(chunk * HALO, HALO)
        for part in range(2):
            patch3[part, rows, :] = joined(
                jnp.dot(split(ext[part, rows, :]), place_t[...], preferred_element_type=F32)
            )

        @pl.loop(0, 4)
        def _(step):
            local = pl.multiple_of(step * 16, 16)
            row = chunk * HALO + local
            pr, pi = probe[0, pl.ds(row, 16), :], probe[1, pl.ds(row, 16), :]
            res, ims = [
                [ext[part, pl.ds(row, 16), c : c + FRAME] for c in FIXED_COLS]
                + [patch3[part, pl.ds(row, 16), :]]
                for part in range(2)
            ]
            for f in range(4):
                xbuf[chunk, pl.ds(f * HALO + local, 16), :FRAME] = (
                    pr * res[f] - pi * ims[f]
                ).astype(BF16)
                xbuf[chunk, pl.ds(f * HALO + local, 16), FRAME:] = (
                    pr * ims[f] + pi * res[f]
                ).astype(BF16)

        half = jnp.dot(xbuf[chunk], inv[...], preferred_element_type=F32).astype(BF16)
        for f in range(4):
            at = f * HALO
            ybuf[f, pl.ds(chunk * HALO, HALO), :] = half[at : at + HALO, :FRAME]
            ybuf[f, pl.ds(FRAME + chunk * HALO, HALO), :] = half[at : at + HALO, FRAME:]

    loads[1].wait()
    loads[2].wait()
    exit_chunk(1)
    exit_chunk(2)

    center = (NG - 1) / 2.0
    half_x = NG // 2
    xpos = lax.broadcasted_iota(jnp.int32, (half_x, LANES), 0).astype(F32) - center
    ypos = lax.broadcasted_iota(jnp.int32, (half_x, LANES), 1).astype(F32) - center

    @pl.loop(0, n_angle)
    def _(a):
        upos = (width - 1) / 2.0 + 2.0 * (xpos * trig[0, a] + ypos * trig[1, a])
        low = jnp.clip(jnp.floor(upos), 0.0, width - 2.0)
        lower_t[a] = low
        frac_t[a] = upos - low

    for copy in halo_copies:
        copy.wait()
    has_above = (me_s > 0).astype(F32)
    has_below = (me_s < n_strip - 1).astype(F32)
    for side, first, present in ((0, 0, has_above), (1, 3 * HALO, has_below)):

        @pl.loop(0, 4)
        def _(step):
            rows = pl.multiple_of(step * 16, 16)
            for part in range(2):
                ext[part, pl.ds(first + rows, 16), :] = (
                    halo_in[side, part, pl.ds(rows, 16), :].astype(F32) * present
                )

    exit_chunk(0)
    exit_chunk(3)

    loads[3].wait()
    loads[4].wait()

    @pl.loop(0, 4)
    def _(f):
        wbuf[...] = jnp.dot(fwd[...], ybuf[f], preferred_element_type=F32)

        @pl.loop(0, FRAME // 16)
        def _(step):
            row = pl.multiple_of(step * 16, 16)
            wr, wi = wbuf[pl.ds(row, 16), :], wbuf[pl.ds(FRAME + row, 16), :]
            measured = amp[f, pl.ds(row, 16), :].astype(F32)
            factor = 1.0 - measured / jnp.sqrt(wr * wr + wi * wi + 1.0)
            mbuf[f, pl.ds(row, 16), :] = (wr * factor).astype(BF16)
            mbuf[f, pl.ds(FRAME + row, 16), :] = (wi * factor).astype(BF16)

        back = jnp.dot(inv[...], mbuf[f], preferred_element_type=F32).astype(BF16)
        for chunk in range(4):
            at = chunk * HALO
            rows = pl.ds(pl.multiple_of(f * HALO, HALO), HALO)
            zbuf[chunk, rows, :FRAME] = back[at : at + HALO]
            zbuf[chunk, rows, FRAME:] = back[FRAME + at : FRAME + at + HALO]

    def place(terms, moved):
        blocks = [moved[:, b * LANES : (b + 1) * LANES] for b in range(width // LANES)]
        for f in range(3):
            b = FIXED_COLS[f] // LANES
            blocks[b] = blocks[b] + terms[f][:, :LANES]
            blocks[b + 1] = blocks[b + 1] + terms[f][:, LANES:]
        return blocks

    def grad_chunk(chunk):
        gbuf[...] = jnp.dot(zbuf[chunk], fwd[...], preferred_element_type=F32)
        rows = pl.ds(chunk * HALO, HALO)
        pr, pi = probe[0, rows, :], probe[1, rows, :]
        gr, gi = gbuf[3 * HALO :, :FRAME], gbuf[3 * HALO :, FRAME:]
        for part, value in ((0, pr * gr + pi * gi), (1, pr * gi - pi * gr)):
            moved3[part] = joined(
                jnp.dot(split(value), place_m[...], preferred_element_type=F32)
            )

        @pl.loop(0, 4)
        def _(step):
            local = pl.multiple_of(step * 16, 16)
            row = chunk * HALO + local
            rows = pl.ds(row, 16)
            pr, pi = probe[0, rows, :], probe[1, rows, :]
            t_re, t_im, q_re, q_im = [], [], 0.0, 0.0
            for f in range(4):
                gr = gbuf[pl.ds(f * HALO + local, 16), :FRAME]
                gi = gbuf[pl.ds(f * HALO + local, 16), FRAME:]
                if f < 3:
                    t_re.append(pr * gr + pi * gi)
                    t_im.append(pr * gi - pi * gr)
                    c = FIXED_COLS[f]
                    er, ei = ext[0, rows, c : c + FRAME], ext[1, rows, c : c + FRAME]
                else:
                    er, ei = patch3[0, rows, :], patch3[1, rows, :]
                q_re = q_re + (er * gr + ei * gi)
                q_im = q_im + (er * gi - ei * gr)
            pterm[pl.ds(row, 16), :] = q_re.astype(BF16)
            pterm[pl.ds(FRAME + row, 16), :] = q_im.astype(BF16)
            for part, terms in ((0, t_re), (1, t_im)):
                for b, value in enumerate(place(terms, moved3[part, pl.ds(local, 16), :])):
                    cols = slice(b * LANES, (b + 1) * LANES)
                    if chunk in (0, 3):
                        grad_out[chunk // 3, part, pl.ds(local, 16), cols] = value.astype(BF16)
                    else:
                        core[part, pl.ds((chunk - 1) * HALO + local, 16), cols] = value

    grad_copies = [
        remote(grad_out.at[1], grad_in.at[0], grad_s.at[0], grad_r.at[0], strip=below),
        remote(grad_out.at[0], grad_in.at[1], grad_s.at[1], grad_r.at[1], strip=above),
    ]
    grad_chunk(0)
    grad_copies[1].start()
    grad_chunk(3)
    grad_copies[0].start()
    grad_chunk(1)
    grad_chunk(2)

    def rs_copy(d):
        peer = lax.rem(me_s + d, n_strip)
        return remote(
            pterm.at[pl.ds(pl.multiple_of(peer * 16, 16), 16)], rs_in.at[d],
            rs_s.at[d], rs_r.at[d], strip=peer,
        )

    @pl.loop(1, n_strip)
    def _(d):
        rs_copy(d).start()

    for copy in grad_copies:
        copy.wait()
    for side, present in ((0, has_above), (1, has_below)):

        @pl.loop(0, 4)
        def _(step):
            local = pl.multiple_of(step * 16, 16)
            rows = pl.ds(side * HALO + local, 16)
            got = [
                core[part, rows, :]
                + grad_in[side, part, pl.ds(local, 16), :].astype(F32) * present
                for part in range(2)
            ]
            core[0, rows, :] = got[0]
            core[1, rows, :] = got[1]
            own = pl.ds(HALO + side * HALO + local, 16)
            phase[rows, :] = (ext[0, own, :] * got[1] - ext[1, own, :] * got[0]).astype(BF16)

    def a2a_copy(d):
        peer = lax.rem(me_a + d, n_angle)
        return remote(
            phase.at[pl.ds(pl.multiple_of(peer * 16, 16), 16)], ph_all.at[me_a],
            a2a_s.at[d], a2a_r.at[d], angle=peer,
        )

    @pl.loop(1, n_angle)
    def _(d):
        a2a_copy(d).start()

    store_og = pltpu.make_async_copy(core, og_hbm, store_sem.at[0])
    store_og.start()
    ph_all[me_a] = phase[pl.ds(pl.multiple_of(me_a * 16, 16), 16), :]

    @pl.loop(1, n_strip)
    def _(d):
        rs_copy(d).wait()

    own_rows = pl.ds(pl.multiple_of(me_s * 16, 16), 16)
    ar_in[me_a] = lax.fori_loop(
        1, n_strip, lambda d, acc: acc + rs_in[d].astype(F32), pterm[own_rows, :].astype(F32)
    )

    def ar_copy(d):
        peer = lax.rem(me_a + d, n_angle)
        return remote(
            ar_in.at[me_a], ar_in.at[me_a], ar_s.at[d], ar_r.at[d], angle=peer
        )

    @pl.loop(1, n_angle)
    def _(d):
        ar_copy(d).start()

    @pl.loop(1, n_angle)
    def _(d):
        a2a_copy(d).wait()

    flip = (
        lax.broadcasted_iota(jnp.int32, (LANES, LANES), 0)
        + lax.broadcasted_iota(jnp.int32, (LANES, LANES), 1)
        == LANES - 1
    ).astype(F32).astype(BF16)

    @pl.loop(0, n_angle)
    def _(a):
        rows = ph_all[a]
        mirrored = [
            jnp.dot(rows[:, b * LANES : (b + 1) * LANES], flip, preferred_element_type=F32)
            for b in range(8)
        ]
        both = jnp.concatenate(
            [rows.astype(F32), jnp.concatenate(mirrored[::-1], axis=1)], axis=0
        )
        lhs[a, :32, :] = both.astype(BF16)
        lhs[a, 32:, :] = pltpu.roll(both, width - 1, 1).astype(BF16)

    column = lax.broadcasted_iota(jnp.int32, (LANES, LANES), 0).astype(F32).astype(BF16)
    one, zero = jnp.ones((), BF16), jnp.zeros((), BF16)

    def project(x):
        total = jnp.zeros((32, LANES), F32)
        for a in range(n_angle):
            low = lower_t[a, pl.ds(x, 1), :] - float(WINDOW[0])
            frac = frac_t[a, pl.ds(x, 1), :]
            picks = jnp.concatenate(
                [
                    jnp.where(column == (low - float(j * LANES)).astype(BF16), one, zero)
                    for j in range((WINDOW[1] - WINDOW[0]) // LANES)
                ],
                axis=0,
            )
            got = jnp.dot(lhs[a, :, WINDOW[0] : WINDOW[1]], picks, preferred_element_type=F32)
            total = total + (got[:32] * (1.0 - frac) + got[32:] * frac)
        vol[:, pl.ds(pl.multiple_of(x * LANES, LANES), LANES)] = total[:16]
        high = total[16:].astype(BF16)
        rest = (total[16:] - high.astype(F32)).astype(BF16)
        turned = jnp.dot(jnp.concatenate([high, rest], axis=0), flip, preferred_element_type=F32)
        vol[:, pl.ds(pl.multiple_of((NG - 1 - x) * LANES, LANES), LANES)] = turned[:16] + turned[16:]

    pl.loop(0, half_x // 2)(project)

    @pl.loop(1, n_angle)
    def _(d):
        ar_copy(d).wait()

    summed = ar_in[0]
    for a in range(1, n_angle):
        summed = summed + ar_in[a]
    ag_in[own_rows, :] = (summed * scale).astype(BF16)

    def ag_copy(d):
        peer = lax.rem(me_s + d, n_strip)
        return remote(
            ag_in.at[own_rows], ag_in.at[own_rows], ag_s.at[d], ag_r.at[d], strip=peer
        )

    @pl.loop(1, n_strip)
    def _(d):
        ag_copy(d).start()

    pl.loop(half_x // 2, half_x)(project)
    store_vol = pltpu.make_async_copy(vol, vol_hbm, store_sem.at[1])
    store_vol.start()

    def ag_arrived(d):
        sender = lax.rem(me_s + n_strip - d, n_strip)
        rows = pl.ds(pl.multiple_of(sender * 16, 16), 16)
        return remote(ag_in.at[rows], ag_in.at[rows], ag_s.at[d], ag_r.at[d], strip=sender)

    @pl.loop(1, n_strip)
    def _(d):
        ag_copy(d).wait_send()
        ag_arrived(d).wait_recv()

    pg_out[...] = ag_in[...].astype(F32)
    store_pg = pltpu.make_async_copy(pg_out, pg_hbm, store_sem.at[2])
    store_pg.start()
    store_og.wait()
    store_vol.wait()
    store_pg.wait()


def shards(object_field, amplitudes, scan_offsets, probe_field, tilt_angles):
    n_angle, n_strip = lax.axis_size("angle"), lax.axis_size("strip")
    width = object_field.shape[3]
    fwd, inv = dft_blocks()
    trig = jnp.stack([jnp.cos(tilt_angles), jnp.sin(tilt_angles)])
    cols = scan_offsets[0, 3:, 1]
    scale = 1.0 / math.sqrt(n_angle * n_strip * scan_offsets.shape[1])
    hbm = pl.BlockSpec(memory_space=pl.ANY)
    smem = pl.BlockSpec(memory_space=pltpu.SMEM)
    vmem, dma = pltpu.VMEM, pltpu.SemaphoreType.DMA
    object_grad, probe_grad, volume = pl.pallas_call(
        lambda *refs: kernel(n_angle, n_strip, scale, *refs),
        out_shape=(
            jax.ShapeDtypeStruct((2, 128, width), F32),
            jax.ShapeDtypeStruct((2 * FRAME, FRAME), F32),
            jax.ShapeDtypeStruct((16, NG * NG), F32),
        ),
        in_specs=[smem, smem] + [hbm] * 5,
        out_specs=(hbm, hbm, hbm),
        scratch_shapes=[
            vmem((2, FRAME, width), F32),
            vmem((2, FRAME, FRAME), F32),
            vmem((4, FRAME, FRAME), BF16),
            vmem((2 * FRAME, 2 * FRAME), BF16),
            vmem((2 * FRAME, 2 * FRAME), BF16),
            vmem((2, 2, HALO, width), BF16),
            vmem((2, 2, HALO, width), BF16),
            vmem((width, FRAME), BF16),
            vmem((FRAME, width), BF16),
            vmem((2, HALO, width), F32),
            vmem((2, FRAME, FRAME), F32),
            vmem((4, 4 * HALO, 2 * FRAME), BF16),
            vmem((4, 2 * FRAME, FRAME), BF16),
            vmem((2 * FRAME, FRAME), F32),
            vmem((4, 2 * FRAME, FRAME), BF16),
            vmem((4, 4 * HALO, 2 * FRAME), BF16),
            vmem((4 * HALO, 2 * FRAME), F32),
            vmem((2, 2, HALO, width), BF16),
            vmem((2, 2, HALO, width), BF16),
            vmem((2, 128, width), F32),
            vmem((128, width), BF16),
            vmem((n_angle, 16, width), BF16),
            vmem((2 * FRAME, FRAME), BF16),
            vmem((n_strip, 16, FRAME), BF16),
            vmem((n_angle, 16, FRAME), F32),
            vmem((2 * FRAME, FRAME), BF16),
            vmem((2 * FRAME, FRAME), F32),
            vmem((n_angle, NG // 2, LANES), F32),
            vmem((n_angle, NG // 2, LANES), F32),
            vmem((n_angle, 64, width), BF16),
            vmem((16, NG * NG), F32),
            dma((5,)), dma((3,)), dma((2,)), dma((2,)), dma((2,)), dma((2,)),
            dma((n_angle,)), dma((n_angle,)), dma((n_strip,)), dma((n_strip,)),
            dma((n_angle,)), dma((n_angle,)), dma((n_strip,)), dma((n_strip,)),
        ],
        compiler_params=pltpu.CompilerParams(
            collective_id=0, has_side_effects=True, vmem_limit_bytes=48 * 1024 * 1024
        ),
        name="gradient_step",
    )(
        cols, trig, object_field[:, 0], amplitudes[0], probe_field, fwd, inv
    )
    return (
        object_grad[:, None],
        probe_grad.reshape(2, FRAME, FRAME),
        volume[None, None],
    )


def solution(mesh):
    return jax.shard_map(
        shards,
        mesh=mesh,
        in_specs=(
            P(None, "angle", "strip", None),
            P("angle", "strip", None, None),
            P("angle", "strip", None),
            P(),
            P(),
        ),
        out_specs=(P(None, "angle", "strip", None), P(), P("strip", "angle", None, None)),
        check_vma=False,
    )
```

```python
import math

import jax
import jax.numpy as jnp
import numpy as np
from jax import lax
from jax.experimental import pallas as pl
from jax.experimental.pallas import tpu as pltpu
from jax.sharding import PartitionSpec as P

FRAME = 256
HALO = 64
NG = 128
LANES = 128
MESH = pl.DeviceIdType.MESH
F32 = jnp.float32
BF16 = jnp.bfloat16
FIXED_COLS = (768, 0, 384)
WINDOW = (320, 704)


def dft_blocks():
    index = np.arange(FRAME)
    angle = 2.0 * np.pi / FRAME * ((index[:, None] * index[None, :]) % FRAME)
    cos_tab = np.cos(angle) / math.sqrt(FRAME)
    sin_tab = np.sin(angle) / math.sqrt(FRAME)
    fwd = np.block([[cos_tab, sin_tab], [-sin_tab, cos_tab]])
    inv = np.block([[cos_tab, -sin_tab], [sin_tab, cos_tab]])
    return jnp.asarray(fwd, BF16), jnp.asarray(inv, BF16)


def kernel(
    n_angle, n_strip, scale,
    offs, trig, obj_hbm, amp_hbm, probe_hbm, fwd_hbm, inv_hbm,
    og_hbm, pg_hbm, vol_hbm,
    ext, probe, amp, fwd, inv,
    halo_out, halo_in, place_t, place_m, moved3, patch3, xbuf, ybuf, wbuf, mbuf, zbuf, gbuf,
    grad_out, grad_in, core, phase, ph_all,
    pterm, rs_in, ar_in, ag_in, pg_out,
    lower_t, frac_t, lhs, vol,
    load_sem, store_sem, halo_s, halo_r, grad_s, grad_r, a2a_s, a2a_r,
    rs_s, rs_r, ar_s, ar_r, ag_s, ag_r, mate_s, mate_r, part_s, part_r,
):
    width = ext.shape[2]
    me_a = lax.axis_index("angle")
    me_s = lax.axis_index("strip")
    above = lax.rem(me_s + n_strip - 1, n_strip)
    below = lax.rem(me_s + 1, n_strip)
    core_at = lax.rem(me_s, 2)
    mate = me_s + 1 - 2 * core_at

    loads = [
        pltpu.make_async_copy(obj_hbm, ext.at[:, pl.ds(HALO, 128), :], load_sem.at[0]),
        pltpu.make_async_copy(probe_hbm, probe, load_sem.at[1]),
        pltpu.make_async_copy(inv_hbm, inv, load_sem.at[2]),
        pltpu.make_async_copy(fwd_hbm, fwd, load_sem.at[3]),
        pltpu.make_async_copy(amp_hbm, amp, load_sem.at[4]),
    ]
    for load in loads:
        load.start()

    barrier = pltpu.get_barrier_semaphore()

    @pl.loop(1, n_strip)
    def _(d):
        pl.semaphore_signal(
            barrier, inc=1, device_id={"strip": lax.rem(me_s + d, n_strip)}, device_id_type=MESH
        )

    @pl.loop(1, n_angle)
    def _(d):
        pl.semaphore_signal(
            barrier, inc=1, device_id={"angle": lax.rem(me_a + d, n_angle)}, device_id_type=MESH
        )

    loads[0].wait()
    for side, first in ((0, HALO), (1, 2 * HALO)):

        @pl.loop(0, 4)
        def _(step):
            rows = pl.multiple_of(step * 16, 16)
            for part in range(2):
                halo_out[side, part, pl.ds(rows, 16), :] = ext[
                    part, pl.ds(first + rows, 16), :
                ].astype(BF16)

    pl.semaphore_wait(barrier, n_strip - 1 + n_angle - 1)

    def remote(src, dst, send, recv, **where):
        return pltpu.make_async_remote_copy(
            src_ref=src, dst_ref=dst, send_sem=send, recv_sem=recv,
            device_id=where, device_id_type=MESH,
        )

    halo_copies = [
        remote(halo_out.at[1], halo_in.at[0], halo_s.at[0], halo_r.at[0], strip=below),
        remote(halo_out.at[0], halo_in.at[1], halo_s.at[1], halo_r.at[1], strip=above),
    ]
    for copy in halo_copies:
        copy.start()

    col = offs[0, 1, 3].astype(F32)
    for b in range(width // LANES):
        at = lax.broadcasted_iota(jnp.int32, (LANES, FRAME), 0) + b * LANES
        of = lax.broadcasted_iota(jnp.int32, (LANES, FRAME), 1)
        place_t[b * LANES : (b + 1) * LANES, :] = ((at - of).astype(F32) == col).astype(F32).astype(BF16)
        at = lax.broadcasted_iota(jnp.int32, (FRAME, LANES), 1) + b * LANES
        of = lax.broadcasted_iota(jnp.int32, (FRAME, LANES), 0)
        place_m[:, b * LANES : (b + 1) * LANES] = ((at - of).astype(F32) == col).astype(F32).astype(BF16)

    def split(value):
        high = value.astype(BF16)
        return jnp.concatenate([high, (value - high.astype(F32)).astype(BF16)], axis=0)

    def joined(product):
        rows = product.shape[0] // 2
        return product[:rows] + product[rows:]

    def exit_chunk(chunk):
        rows = pl.ds(chunk * HALO, HALO)
        for part in range(2):
            patch3[part, rows, :] = joined(
                jnp.dot(split(ext[part, rows, :]), place_t[...], preferred_element_type=F32)
            )

        @pl.loop(0, 4)
        def _(step):
            local = pl.multiple_of(step * 16, 16)
            row = chunk * HALO + local
            pr, pi = probe[0, pl.ds(row, 16), :], probe[1, pl.ds(row, 16), :]
            res, ims = [
                [ext[part, pl.ds(row, 16), c : c + FRAME] for c in FIXED_COLS]
                + [patch3[part, pl.ds(row, 16), :]]
                for part in range(2)
            ]
            for f in range(4):
                xbuf[chunk, pl.ds(f * HALO + local, 16), :FRAME] = (
                    pr * res[f] - pi * ims[f]
                ).astype(BF16)
                xbuf[chunk, pl.ds(f * HALO + local, 16), FRAME:] = (
                    pr * ims[f] + pi * res[f]
                ).astype(BF16)

        half = jnp.dot(xbuf[chunk], inv[...], preferred_element_type=F32).astype(BF16)
        for f in range(4):
            at = f * HALO
            ybuf[f, pl.ds(chunk * HALO, HALO), :] = half[at : at + HALO, :FRAME]
            ybuf[f, pl.ds(FRAME + chunk * HALO, HALO), :] = half[at : at + HALO, FRAME:]

    loads[1].wait()
    loads[2].wait()
    exit_chunk(1)
    exit_chunk(2)

    center = (NG - 1) / 2.0
    n_rows = NG // 4
    first_row = core_at * n_rows
    shape = (n_rows, LANES)
    xpos = (lax.broadcasted_iota(jnp.int32, shape, 0) + first_row).astype(F32) - center
    ypos = lax.broadcasted_iota(jnp.int32, shape, 1).astype(F32) - center

    @pl.loop(0, n_angle)
    def _(a):
        upos = (width - 1) / 2.0 + 2.0 * (xpos * trig[0, a] + ypos * trig[1, a])
        low = jnp.clip(jnp.floor(upos), 0.0, width - 2.0)
        lower_t[a] = low - float(WINDOW[0])
        frac_t[a] = upos - low

    for copy in halo_copies:
        copy.wait()
    has_above = (me_s > 0).astype(F32)
    has_below = (me_s < n_strip - 1).astype(F32)
    for side, first, present in ((0, 0, has_above), (1, 3 * HALO, has_below)):

        @pl.loop(0, 4)
        def _(step):
            rows = pl.multiple_of(step * 16, 16)
            for part in range(2):
                ext[part, pl.ds(first + rows, 16), :] = (
                    halo_in[side, part, pl.ds(rows, 16), :].astype(F32) * present
                )

    exit_chunk(0)
    exit_chunk(3)

    loads[3].wait()
    loads[4].wait()

    @pl.loop(0, 4)
    def _(f):
        wbuf[...] = jnp.dot(fwd[...], ybuf[f], preferred_element_type=F32)

        @pl.loop(0, FRAME // 16)
        def _(step):
            row = pl.multiple_of(step * 16, 16)
            wr, wi = wbuf[pl.ds(row, 16), :], wbuf[pl.ds(FRAME + row, 16), :]
            measured = amp[f, pl.ds(row, 16), :].astype(F32)
            factor = 1.0 - measured * lax.rsqrt(wr * wr + wi * wi + 1.0)
            mbuf[f, pl.ds(row, 16), :] = (wr * factor).astype(BF16)
            mbuf[f, pl.ds(FRAME + row, 16), :] = (wi * factor).astype(BF16)

        back = jnp.dot(inv[...], mbuf[f], preferred_element_type=F32).astype(BF16)
        for chunk in range(4):
            at = chunk * HALO
            rows = pl.ds(pl.multiple_of(f * HALO, HALO), HALO)
            zbuf[chunk, rows, :FRAME] = back[at : at + HALO]
            zbuf[chunk, rows, FRAME:] = back[FRAME + at : FRAME + at + HALO]

    def place(terms, moved):
        blocks = [moved[:, b * LANES : (b + 1) * LANES] for b in range(width // LANES)]
        for f in range(3):
            b = FIXED_COLS[f] // LANES
            blocks[b] = blocks[b] + terms[f][:, :LANES]
            blocks[b + 1] = blocks[b + 1] + terms[f][:, LANES:]
        return blocks

    def grad_chunk(chunk):
        gbuf[...] = jnp.dot(zbuf[chunk], fwd[...], preferred_element_type=F32)
        rows = pl.ds(chunk * HALO, HALO)
        pr, pi = probe[0, rows, :], probe[1, rows, :]
        gr, gi = gbuf[3 * HALO :, :FRAME], gbuf[3 * HALO :, FRAME:]
        for part, value in ((0, pr * gr + pi * gi), (1, pr * gi - pi * gr)):
            moved3[part] = joined(
                jnp.dot(split(value), place_m[...], preferred_element_type=F32)
            )

        @pl.loop(0, 4)
        def _(step):
            local = pl.multiple_of(step * 16, 16)
            row = chunk * HALO + local
            rows = pl.ds(row, 16)
            pr, pi = probe[0, rows, :], probe[1, rows, :]
            t_re, t_im, q_re, q_im = [], [], 0.0, 0.0
            for f in range(4):
                gr = gbuf[pl.ds(f * HALO + local, 16), :FRAME]
                gi = gbuf[pl.ds(f * HALO + local, 16), FRAME:]
                if f < 3:
                    t_re.append(pr * gr + pi * gi)
                    t_im.append(pr * gi - pi * gr)
                    c = FIXED_COLS[f]
                    er, ei = ext[0, rows, c : c + FRAME], ext[1, rows, c : c + FRAME]
                else:
                    er, ei = patch3[0, rows, :], patch3[1, rows, :]
                q_re = q_re + (er * gr + ei * gi)
                q_im = q_im + (er * gi - ei * gr)
            pterm[pl.ds(row, 16), :] = q_re.astype(BF16)
            pterm[pl.ds(FRAME + row, 16), :] = q_im.astype(BF16)
            for part, terms in ((0, t_re), (1, t_im)):
                for b, value in enumerate(place(terms, moved3[part, pl.ds(local, 16), :])):
                    cols = slice(b * LANES, (b + 1) * LANES)
                    if chunk in (0, 3):
                        grad_out[chunk // 3, part, pl.ds(local, 16), cols] = value.astype(BF16)
                    else:
                        core[part, pl.ds((chunk - 1) * HALO + local, 16), cols] = value

    grad_copies = [
        remote(grad_out.at[1], grad_in.at[0], grad_s.at[0], grad_r.at[0], strip=below),
        remote(grad_out.at[0], grad_in.at[1], grad_s.at[1], grad_r.at[1], strip=above),
    ]
    grad_chunk(0)
    grad_copies[1].start()
    grad_chunk(3)
    grad_copies[0].start()
    grad_chunk(1)
    grad_chunk(2)

    def rs_copy(d):
        peer = lax.rem(me_s + d, n_strip)
        return remote(
            pterm.at[pl.ds(pl.multiple_of(peer * 16, 16), 16)], rs_in.at[d],
            rs_s.at[d], rs_r.at[d], strip=peer,
        )

    around = (WINDOW[0] // LANES * LANES, -(-WINDOW[1] // LANES) * LANES)
    for copy in grad_copies:
        copy.wait()
    for side, present in ((0, has_above), (1, has_below)):

        @pl.loop(0, 4)
        def _(step):
            local = pl.multiple_of(step * 16, 16)
            rows = pl.ds(side * HALO + local, 16)
            got = [
                core[part, rows, :]
                + grad_in[side, part, pl.ds(local, 16), :].astype(F32) * present
                for part in range(2)
            ]
            core[0, rows, :] = got[0]
            core[1, rows, :] = got[1]
            own = pl.ds(HALO + side * HALO + local, 16)
            cut = slice(around[0], around[1])
            value = ext[0, own, cut] * got[1][:, cut] - ext[1, own, cut] * got[0][:, cut]
            value = pltpu.roll(value, around[1] - WINDOW[0], 1)
            phase[rows, :] = value[:, : WINDOW[1] - WINDOW[0]].astype(BF16)

    def a2a_copy(d):
        peer = lax.rem(me_a + d, n_angle)
        return remote(
            phase.at[pl.ds(pl.multiple_of(peer * 16, 16), 16)], ph_all.at[core_at, me_a],
            a2a_s.at[d], a2a_r.at[d], angle=peer,
        )

    def mate_copy(d):
        at = ph_all.at[core_at, lax.rem(me_a + n_angle - d, n_angle)]
        return remote(at, at, mate_s.at[d], mate_r.at[d], strip=mate)

    @pl.loop(1, n_angle)
    def _(d):
        a2a_copy(d).start()

    ph_all[core_at, me_a] = phase[pl.ds(pl.multiple_of(me_a * 16, 16), 16), :]
    mate_copy(0).start()

    @pl.loop(1, n_strip)
    def _(d):
        rs_copy(d).start()

    store_og = pltpu.make_async_copy(core, og_hbm, store_sem.at[0])
    store_og.start()

    @pl.loop(1, n_angle)
    def _(d):
        a2a_copy(d).wait()
        mate_copy(d).start()

    @pl.loop(1, n_strip)
    def _(d):
        rs_copy(d).wait()

    own_rows = pl.ds(pl.multiple_of(me_s * 16, 16), 16)
    ar_in[me_a] = lax.fori_loop(
        1, n_strip, lambda d, acc: acc + rs_in[d].astype(F32), pterm[own_rows, :].astype(F32)
    )

    def ar_copy(d):
        peer = lax.rem(me_a + d, n_angle)
        return remote(
            ar_in.at[me_a], ar_in.at[me_a], ar_s.at[d], ar_r.at[d], angle=peer
        )

    @pl.loop(1, n_angle)
    def _(d):
        ar_copy(d).start()

    @pl.loop(0, n_angle)
    def _(d):
        mate_copy(d).wait()

    flip = (
        lax.broadcasted_iota(jnp.int32, (LANES, LANES), 0)
        + lax.broadcasted_iota(jnp.int32, (LANES, LANES), 1)
        == LANES - 1
    ).astype(F32).astype(BF16)
    n_cols = WINDOW[1] - WINDOW[0]

    @pl.loop(0, n_angle)
    def _(a):
        rows = jnp.concatenate([ph_all[0, a], ph_all[1, a]], axis=0)
        mirrored = [
            jnp.dot(rows[:, b : b + LANES], flip, preferred_element_type=F32)
            for b in range(0, n_cols, LANES)
        ]
        both = jnp.concatenate(
            [rows.astype(F32), jnp.concatenate(mirrored[::-1], axis=1)], axis=0
        )
        lhs[a, :64, :] = both.astype(BF16)
        lhs[a, 64:, :] = pltpu.roll(both, n_cols - 1, 1).astype(BF16)

    column = lax.broadcasted_iota(jnp.int32, (LANES, LANES), 0).astype(F32).astype(BF16)
    one, zero = jnp.ones((), BF16), jnp.zeros((), BF16)

    def one_hot(a, i):
        low = lower_t[a, pl.ds(i, 1), :]
        return jnp.concatenate(
            [
                jnp.where(column == (low - float(j)).astype(BF16), one, zero)
                for j in range(0, n_cols, LANES)
            ],
            axis=0,
        )

    def project(pair):
        totals = [jnp.zeros((64, LANES), F32) for _ in range(2)]
        for a in range(n_angle):
            picks = jnp.concatenate([one_hot(a, 2 * pair + k) for k in range(2)], axis=1)
            got = jnp.dot(lhs[a], picks, preferred_element_type=F32)
            for k in range(2):
                frac = frac_t[a, pl.ds(2 * pair + k, 1), :]
                part = got[:, k * LANES : (k + 1) * LANES]
                totals[k] = totals[k] + (part[:64] * (1.0 - frac) + part[64:] * frac)
        for k in range(2):
            x = first_row + 2 * pair + k
            turned = joined(
                jnp.dot(split(totals[k][32:]), flip, preferred_element_type=F32)
            )
            here = pl.ds(pl.multiple_of(x * LANES, LANES), LANES)
            there = pl.ds(pl.multiple_of((NG - 1 - x) * LANES, LANES), LANES)
            for c in range(2):
                vol[c, :, here] = totals[k][c * 16 : c * 16 + 16]
                vol[c, :, there] = turned[c * 16 : c * 16 + 16]

    part_cols = n_rows // 2 * LANES

    def part_at(owner, half, side):
        row = owner * n_rows + half * (n_rows // 2)
        if side:
            row = NG - row - n_rows // 2
        return pl.ds(pl.multiple_of(row * LANES, LANES), part_cols)

    def part_copy(half, side):
        at = vol.at[1 - core_at, :, part_at(core_at, half, side)]
        return remote(at, at, part_s.at[half, side], part_r.at[half, side], strip=mate)

    def part_arrived(half, side):
        at = vol.at[core_at, :, part_at(1 - core_at, half, side)]
        return remote(at, at, part_s.at[half, side], part_r.at[half, side], strip=mate)

    pl.loop(0, n_rows // 4)(project)
    for side in range(2):
        part_copy(0, side).start()

    @pl.loop(1, n_angle)
    def _(d):
        ar_copy(d).wait()

    summed = ar_in[0]
    for a in range(1, n_angle):
        summed = summed + ar_in[a]
    ag_in[own_rows, :] = (summed * scale).astype(BF16)

    def ag_copy(d):
        peer = lax.rem(me_s + d, n_strip)
        return remote(
            ag_in.at[own_rows], ag_in.at[own_rows], ag_s.at[d], ag_r.at[d], strip=peer
        )

    @pl.loop(1, n_strip)
    def _(d):
        ag_copy(d).start()

    pl.loop(n_rows // 4, n_rows // 2)(project)
    for side in range(2):
        part_copy(1, side).start()

    def ag_arrived(d):
        sender = lax.rem(me_s + n_strip - d, n_strip)
        rows = pl.ds(pl.multiple_of(sender * 16, 16), 16)
        return remote(ag_in.at[rows], ag_in.at[rows], ag_s.at[d], ag_r.at[d], strip=sender)

    @pl.loop(1, n_strip)
    def _(d):
        ag_copy(d).wait_send()
        ag_arrived(d).wait_recv()

    pg_out[...] = ag_in[...].astype(F32)
    store_pg = pltpu.make_async_copy(pg_out, pg_hbm, store_sem.at[2])
    store_pg.start()
    for half in range(2):
        for side in range(2):
            part_copy(half, side).wait_send()
            part_arrived(half, side).wait_recv()
    store_vol = pltpu.make_async_copy(vol.at[core_at], vol_hbm, store_sem.at[1])
    store_vol.start()
    store_og.wait()
    store_pg.wait()
    store_vol.wait()


def shards(object_field, amplitudes, scan_offsets, probe_field, tilt_angles):
    n_angle, n_strip = lax.axis_size("angle"), lax.axis_size("strip")
    width = object_field.shape[3]
    fwd, inv = dft_blocks()
    trig = jnp.stack([jnp.cos(tilt_angles), jnp.sin(tilt_angles)])
    scale = 1.0 / math.sqrt(n_angle * n_strip * scan_offsets.shape[1])
    n_cols = WINDOW[1] - WINDOW[0]
    hbm = pl.BlockSpec(memory_space=pltpu.HBM)
    smem = pl.BlockSpec(memory_space=pltpu.SMEM)
    vmem, dma = pltpu.VMEM, pltpu.SemaphoreType.DMA
    object_grad, probe_grad, volume = pl.pallas_call(
        lambda *refs: kernel(n_angle, n_strip, scale, *refs),
        out_shape=(
            jax.ShapeDtypeStruct((2, 128, width), F32),
            jax.ShapeDtypeStruct((2 * FRAME, FRAME), F32),
            jax.ShapeDtypeStruct((16, NG * NG), F32),
        ),
        in_specs=[smem, smem] + [hbm] * 5,
        out_specs=(hbm, hbm, hbm),
        scratch_shapes=[
            vmem((2, FRAME, width), F32),
            vmem((2, FRAME, FRAME), F32),
            vmem((4, FRAME, FRAME), BF16),
            vmem((2 * FRAME, 2 * FRAME), BF16),
            vmem((2 * FRAME, 2 * FRAME), BF16),
            vmem((2, 2, HALO, width), BF16),
            vmem((2, 2, HALO, width), BF16),
            vmem((width, FRAME), BF16),
            vmem((FRAME, width), BF16),
            vmem((2, HALO, width), F32),
            vmem((2, FRAME, FRAME), F32),
            vmem((4, 4 * HALO, 2 * FRAME), BF16),
            vmem((4, 2 * FRAME, FRAME), BF16),
            vmem((2 * FRAME, FRAME), F32),
            vmem((4, 2 * FRAME, FRAME), BF16),
            vmem((4, 4 * HALO, 2 * FRAME), BF16),
            vmem((4 * HALO, 2 * FRAME), F32),
            vmem((2, 2, HALO, width), BF16),
            vmem((2, 2, HALO, width), BF16),
            vmem((2, 128, width), F32),
            vmem((128, n_cols), BF16),
            vmem((2, n_angle, 16, n_cols), BF16),
            vmem((2 * FRAME, FRAME), BF16),
            vmem((n_strip, 16, FRAME), BF16),
            vmem((n_angle, 16, FRAME), F32),
            vmem((2 * FRAME, FRAME), BF16),
            vmem((2 * FRAME, FRAME), F32),
            vmem((n_angle, NG // 4, LANES), F32),
            vmem((n_angle, NG // 4, LANES), F32),
            vmem((n_angle, 128, n_cols), BF16),
            vmem((2, 16, NG * NG), F32),
            dma((5,)), dma((3,)), dma((2,)), dma((2,)), dma((2,)), dma((2,)),
            dma((n_angle,)), dma((n_angle,)), dma((n_strip,)), dma((n_strip,)),
            dma((n_angle,)), dma((n_angle,)), dma((n_strip,)), dma((n_strip,)),
            dma((n_angle,)), dma((n_angle,)), dma((2, 2)), dma((2, 2)),
        ],
        compiler_params=pltpu.CompilerParams(
            collective_id=0, has_side_effects=True, vmem_limit_bytes=60 * 1024 * 1024
        ),
        name="gradient_step",
    )(
        scan_offsets.transpose(0, 2, 1), trig, object_field[:, 0], amplitudes[0], probe_field, fwd, inv
    )
    return (
        object_grad[:, None],
        probe_grad.reshape(2, FRAME, FRAME),
        volume[None, None],
    )


def solution(mesh):
    return jax.shard_map(
        shards,
        mesh=mesh,
        in_specs=(
            P(None, "angle", "strip", None),
            P("angle", "strip", None, None),
            P("angle", "strip", None),
            P(),
            P(),
        ),
        out_specs=(P(None, "angle", "strip", None), P(), P("strip", "angle", None, None)),
        check_vma=False,
    )
```

```python
import math

import jax
import jax.numpy as jnp
import numpy as np
from jax import lax
from jax.experimental import pallas as pl
from jax.experimental.pallas import tpu as pltpu
from jax.sharding import PartitionSpec as P

FRAME = 256
HALO = 64
NG = 128
LANES = 128
MESH = pl.DeviceIdType.MESH
F32 = jnp.float32
BF16 = jnp.bfloat16
FIXED_COLS = (768, 0, 384)
WINDOW = (320, 704)


def dft_blocks():
    index = np.arange(FRAME)
    angle = 2.0 * np.pi / FRAME * ((index[:, None] * index[None, :]) % FRAME)
    cos_tab = np.cos(angle) / math.sqrt(FRAME)
    sin_tab = np.sin(angle) / math.sqrt(FRAME)
    fwd = np.block([[cos_tab, sin_tab], [-sin_tab, cos_tab]])
    inv = np.block([[cos_tab, -sin_tab], [sin_tab, cos_tab]])
    return jnp.asarray(fwd, BF16), jnp.asarray(inv, BF16)


def kernel(
    n_angle, n_strip, scale,
    offs, trig, obj_hbm, amp_hbm, probe_hbm, fwd_hbm, inv_hbm,
    og_hbm, pg_hbm, vol_hbm,
    ext, probe, amp, fwd, inv,
    halo_out, halo_in, place_t, place_m, moved3, patch3, xbuf, ybuf, wbuf, mbuf, zbuf, gbuf,
    grad_out, grad_in, core, phase, ph_all,
    pterm, rs_in, ar_in, ag_in, pg_out,
    lower_t, frac_t, lhs, total, vol,
    load_sem, store_sem, halo_s, halo_r, grad_s, grad_r, a2a_s, a2a_r,
    rs_s, rs_r, ar_s, ar_r, ag_s, ag_r, mate_s, mate_r, part_s, part_r, own_sem, mate_sem,
):
    width = ext.shape[2]
    me_a = lax.axis_index("angle")
    me_s = lax.axis_index("strip")
    above = lax.rem(me_s + n_strip - 1, n_strip)
    below = lax.rem(me_s + 1, n_strip)
    core_at = lax.rem(me_s, 2)
    mate = me_s + 1 - 2 * core_at

    loads = [
        pltpu.make_async_copy(obj_hbm, ext.at[:, pl.ds(HALO, 128), :], load_sem.at[0]),
        pltpu.make_async_copy(probe_hbm, probe, load_sem.at[1]),
        pltpu.make_async_copy(inv_hbm, inv, load_sem.at[2]),
        pltpu.make_async_copy(fwd_hbm, fwd, load_sem.at[3]),
        pltpu.make_async_copy(amp_hbm, amp, load_sem.at[4]),
    ]
    for load in loads:
        load.start()

    barrier = pltpu.get_barrier_semaphore()

    @pl.loop(1, n_strip)
    def _(d):
        pl.semaphore_signal(
            barrier, inc=1, device_id={"strip": lax.rem(me_s + d, n_strip)}, device_id_type=MESH
        )

    @pl.loop(1, n_angle)
    def _(d):
        pl.semaphore_signal(
            barrier, inc=1, device_id={"angle": lax.rem(me_a + d, n_angle)}, device_id_type=MESH
        )

    loads[0].wait()
    for side, first in ((0, HALO), (1, 2 * HALO)):

        @pl.loop(0, 4)
        def _(step):
            rows = pl.multiple_of(step * 16, 16)
            for part in range(2):
                halo_out[side, part, pl.ds(rows, 16), :] = ext[
                    part, pl.ds(first + rows, 16), :
                ].astype(BF16)

    pl.semaphore_wait(barrier, n_strip - 1 + n_angle - 1)

    def remote(src, dst, send, recv, **where):
        return pltpu.make_async_remote_copy(
            src_ref=src, dst_ref=dst, send_sem=send, recv_sem=recv,
            device_id=where, device_id_type=MESH,
        )

    halo_copies = [
        remote(halo_out.at[1], halo_in.at[0], halo_s.at[0], halo_r.at[0], strip=below),
        remote(halo_out.at[0], halo_in.at[1], halo_s.at[1], halo_r.at[1], strip=above),
    ]
    for copy in halo_copies:
        copy.start()

    col = offs[0, 1, 3].astype(F32)
    for b in range(width // LANES):
        at = lax.broadcasted_iota(jnp.int32, (LANES, FRAME), 0) + b * LANES
        of = lax.broadcasted_iota(jnp.int32, (LANES, FRAME), 1)
        place_t[b * LANES : (b + 1) * LANES, :] = ((at - of).astype(F32) == col).astype(F32).astype(BF16)
        at = lax.broadcasted_iota(jnp.int32, (FRAME, LANES), 1) + b * LANES
        of = lax.broadcasted_iota(jnp.int32, (FRAME, LANES), 0)
        place_m[:, b * LANES : (b + 1) * LANES] = ((at - of).astype(F32) == col).astype(F32).astype(BF16)

    def split(value):
        high = value.astype(BF16)
        return jnp.concatenate([high, (value - high.astype(F32)).astype(BF16)], axis=0)

    def joined(product):
        rows = product.shape[0] // 2
        return product[:rows] + product[rows:]

    def exit_chunk(chunk):
        rows = pl.ds(chunk * HALO, HALO)
        for part in range(2):
            patch3[part, rows, :] = joined(
                jnp.dot(split(ext[part, rows, :]), place_t[...], preferred_element_type=F32)
            )

        @pl.loop(0, 4)
        def _(step):
            local = pl.multiple_of(step * 16, 16)
            row = chunk * HALO + local
            pr, pi = probe[0, pl.ds(row, 16), :], probe[1, pl.ds(row, 16), :]
            res, ims = [
                [ext[part, pl.ds(row, 16), c : c + FRAME] for c in FIXED_COLS]
                + [patch3[part, pl.ds(row, 16), :]]
                for part in range(2)
            ]
            for f in range(4):
                xbuf[chunk, pl.ds(f * HALO + local, 16), :FRAME] = (
                    pr * res[f] - pi * ims[f]
                ).astype(BF16)
                xbuf[chunk, pl.ds(f * HALO + local, 16), FRAME:] = (
                    pr * ims[f] + pi * res[f]
                ).astype(BF16)

        half = jnp.dot(xbuf[chunk], inv[...], preferred_element_type=F32).astype(BF16)
        for f in range(4):
            at = f * HALO
            ybuf[f, pl.ds(chunk * HALO, HALO), :] = half[at : at + HALO, :FRAME]
            ybuf[f, pl.ds(FRAME + chunk * HALO, HALO), :] = half[at : at + HALO, FRAME:]

    loads[1].wait()
    loads[2].wait()
    exit_chunk(1)
    exit_chunk(2)

    center = (NG - 1) / 2.0
    n_rows = NG // 4
    first_row = core_at * n_rows
    shape = (n_rows, LANES)
    xpos = (lax.broadcasted_iota(jnp.int32, shape, 0) + first_row).astype(F32) - center
    ypos = lax.broadcasted_iota(jnp.int32, shape, 1).astype(F32) - center

    @pl.loop(0, n_angle)
    def _(a):
        upos = (width - 1) / 2.0 + 2.0 * (xpos * trig[0, a] + ypos * trig[1, a])
        low = jnp.clip(jnp.floor(upos), 0.0, width - 2.0)
        lower_t[a] = low - float(WINDOW[0])
        total[pl.ds(a * (n_rows // n_angle), n_rows // n_angle)] = jnp.zeros(
            (n_rows // n_angle, 64, LANES), F32
        )
        frac_t[a] = upos - low

    for copy in halo_copies:
        copy.wait()
    has_above = (me_s > 0).astype(F32)
    has_below = (me_s < n_strip - 1).astype(F32)
    for side, first, present in ((0, 0, has_above), (1, 3 * HALO, has_below)):

        @pl.loop(0, 4)
        def _(step):
            rows = pl.multiple_of(step * 16, 16)
            for part in range(2):
                ext[part, pl.ds(first + rows, 16), :] = (
                    halo_in[side, part, pl.ds(rows, 16), :].astype(F32) * present
                )

    exit_chunk(0)
    exit_chunk(3)

    loads[3].wait()
    loads[4].wait()

    def misfit(f, rows):
        wr, wi = wbuf[f, rows, :], wbuf[f, rows.start + FRAME : rows.stop + FRAME, :]
        measured = amp[f, rows, :].astype(F32)
        factor = 1.0 - measured * lax.rsqrt(wr * wr + wi * wi + 1.0)
        mbuf[f, rows, :] = (wr * factor).astype(BF16)
        mbuf[f, rows.start + FRAME : rows.stop + FRAME, :] = (wi * factor).astype(BF16)

    for f in range(4):
        wbuf[f] = jnp.dot(fwd[...], ybuf[f], preferred_element_type=F32)
        for row in range(0, FRAME, 32):
            misfit(f, slice(row, row + 32))
    for f in range(4):
        back = jnp.dot(inv[...], mbuf[f], preferred_element_type=F32).astype(BF16)
        for chunk in range(4):
            at = chunk * HALO
            zbuf[chunk, f * HALO : (f + 1) * HALO, :FRAME] = back[at : at + HALO]
            zbuf[chunk, f * HALO : (f + 1) * HALO, FRAME:] = back[FRAME + at : FRAME + at + HALO]

    def place(terms, moved):
        blocks = [moved[:, b * LANES : (b + 1) * LANES] for b in range(width // LANES)]
        for f in range(3):
            b = FIXED_COLS[f] // LANES
            blocks[b] = blocks[b] + terms[f][:, :LANES]
            blocks[b + 1] = blocks[b + 1] + terms[f][:, LANES:]
        return blocks

    def grad_chunk(chunk):
        gbuf[...] = jnp.dot(zbuf[chunk], fwd[...], preferred_element_type=F32)
        rows = pl.ds(chunk * HALO, HALO)
        pr, pi = probe[0, rows, :], probe[1, rows, :]
        gr, gi = gbuf[3 * HALO :, :FRAME], gbuf[3 * HALO :, FRAME:]
        for part, value in ((0, pr * gr + pi * gi), (1, pr * gi - pi * gr)):
            moved3[part] = joined(
                jnp.dot(split(value), place_m[...], preferred_element_type=F32)
            )

        @pl.loop(0, 4)
        def _(step):
            local = pl.multiple_of(step * 16, 16)
            row = chunk * HALO + local
            rows = pl.ds(row, 16)
            pr, pi = probe[0, rows, :], probe[1, rows, :]
            t_re, t_im, q_re, q_im = [], [], 0.0, 0.0
            for f in range(4):
                gr = gbuf[pl.ds(f * HALO + local, 16), :FRAME]
                gi = gbuf[pl.ds(f * HALO + local, 16), FRAME:]
                if f < 3:
                    t_re.append(pr * gr + pi * gi)
                    t_im.append(pr * gi - pi * gr)
                    c = FIXED_COLS[f]
                    er, ei = ext[0, rows, c : c + FRAME], ext[1, rows, c : c + FRAME]
                else:
                    er, ei = patch3[0, rows, :], patch3[1, rows, :]
                q_re = q_re + (er * gr + ei * gi)
                q_im = q_im + (er * gi - ei * gr)
            pterm[pl.ds(row, 16), :] = q_re.astype(BF16)
            pterm[pl.ds(FRAME + row, 16), :] = q_im.astype(BF16)
            for part, terms in ((0, t_re), (1, t_im)):
                for b, value in enumerate(place(terms, moved3[part, pl.ds(local, 16), :])):
                    cols = slice(b * LANES, (b + 1) * LANES)
                    if chunk in (0, 3):
                        grad_out[chunk // 3, part, pl.ds(local, 16), cols] = value.astype(BF16)
                    else:
                        core[part, pl.ds((chunk - 1) * HALO + local, 16), cols] = value

    grad_copies = [
        remote(grad_out.at[1], grad_in.at[0], grad_s.at[0], grad_r.at[0], strip=below),
        remote(grad_out.at[0], grad_in.at[1], grad_s.at[1], grad_r.at[1], strip=above),
    ]
    grad_chunk(0)
    grad_copies[1].start()
    grad_chunk(3)
    grad_copies[0].start()
    grad_chunk(1)
    grad_chunk(2)

    def rs_copy(d):
        peer = lax.rem(me_s + d, n_strip)
        return remote(
            pterm.at[pl.ds(pl.multiple_of(peer * 16, 16), 16)], rs_in.at[d],
            rs_s.at[d], rs_r.at[d], strip=peer,
        )

    @pl.loop(1, n_strip)
    def _(d):
        rs_copy(d).start()

    around = (WINDOW[0] // LANES * LANES, -(-WINDOW[1] // LANES) * LANES)
    for copy in grad_copies:
        copy.wait()
    for side, present in ((0, has_above), (1, has_below)):

        @pl.loop(0, 4)
        def _(step):
            local = pl.multiple_of(step * 16, 16)
            rows = pl.ds(side * HALO + local, 16)
            got = [
                core[part, rows, :]
                + grad_in[side, part, pl.ds(local, 16), :].astype(F32) * present
                for part in range(2)
            ]
            core[0, rows, :] = got[0]
            core[1, rows, :] = got[1]
            own = pl.ds(HALO + side * HALO + local, 16)
            cut = slice(around[0], around[1])
            value = ext[0, own, cut] * got[1][:, cut] - ext[1, own, cut] * got[0][:, cut]
            value = pltpu.roll(value, around[1] - WINDOW[0], 1)
            phase[rows, :] = value[:, : WINDOW[1] - WINDOW[0]].astype(BF16)

    def farness(step):
        near = (step + 1) // 2
        return jnp.where(lax.rem(step, 2) == 1, near, lax.rem(n_angle - near, n_angle))

    def a2a_copy(d):
        peer = lax.rem(me_a + d, n_angle)
        return remote(
            phase.at[pl.ds(pl.multiple_of(peer * 16, 16), 16)], ph_all.at[core_at, me_a],
            a2a_s.at[d], a2a_r.at[d], angle=peer,
        )

    def cross_copy(d):
        peer = lax.rem(me_a + d, n_angle)
        return remote(
            phase.at[pl.ds(pl.multiple_of(peer * 16, 16), 16)], ph_all.at[core_at, me_a],
            mate_s.at[d], mate_r.at[d], angle=peer, strip=mate,
        )

    @pl.loop(0, n_angle - 1)
    def _(step):
        d = farness(n_angle - 1 - step)
        a2a_copy(d).start()
        cross_copy(d).start()

    cross_copy(0).start()
    ph_all[core_at, me_a] = phase[pl.ds(pl.multiple_of(me_a * 16, 16), 16), :]

    store_og = pltpu.make_async_copy(core, og_hbm, store_sem.at[0])
    store_og.start()

    @pl.loop(1, n_strip)
    def _(d):
        rs_copy(d).wait()

    own_rows = pl.ds(pl.multiple_of(me_s * 16, 16), 16)
    ar_in[me_a] = lax.fori_loop(
        1, n_strip, lambda d, acc: acc + rs_in[d].astype(F32), pterm[own_rows, :].astype(F32)
    ).astype(BF16)

    def ar_copy(d):
        peer = lax.rem(me_a + d, n_angle)
        return remote(
            ar_in.at[me_a], ar_in.at[me_a], ar_s.at[d], ar_r.at[d], angle=peer
        )

    @pl.loop(1, n_angle)
    def _(d):
        ar_copy(d).start()

    flip = (
        lax.broadcasted_iota(jnp.int32, (LANES, LANES), 0)
        + lax.broadcasted_iota(jnp.int32, (LANES, LANES), 1)
        == LANES - 1
    ).astype(F32).astype(BF16)
    n_cols = WINDOW[1] - WINDOW[0]
    column = lax.broadcasted_iota(jnp.int32, (LANES, LANES), 0).astype(F32).astype(BF16)
    one, zero = jnp.ones((), BF16), jnp.zeros((), BF16)

    def ag_copy(d):
        peer = lax.rem(me_s + d, n_strip)
        return remote(
            ag_in.at[own_rows], ag_in.at[own_rows], ag_s.at[d], ag_r.at[d], strip=peer
        )

    def gather_probe():
        @pl.loop(1, n_angle)
        def _(d):
            ar_copy(d).wait()

        summed = ar_in[0].astype(F32)
        for a in range(1, n_angle):
            summed = summed + ar_in[a].astype(F32)
        ag_in[own_rows, :] = (summed * scale).astype(BF16)

        @pl.loop(1, n_strip)
        def _(d):
            ag_copy(d).start()

    def one_hot(a, i):
        low = lower_t[a, pl.ds(i, 1), :]
        return jnp.concatenate(
            [
                jnp.where(column == (low - float(j)).astype(BF16), one, zero)
                for j in range(0, n_cols, LANES)
            ],
            axis=0,
        )

    def project(a, pair):
        picks = jnp.concatenate([one_hot(a, 2 * pair + k) for k in range(2)], axis=1)
        got = jnp.dot(lhs[...], picks, preferred_element_type=F32)
        for k in range(2):
            frac = frac_t[a, pl.ds(2 * pair + k, 1), :]
            part = got[:, k * LANES : (k + 1) * LANES]
            total[2 * pair + k] += part[:64] * (1.0 - frac) + part[64:] * frac

    @pl.loop(0, n_angle)
    def _(step):
        d = farness(step)
        a = lax.rem(me_a + n_angle - d, n_angle)

        @pl.when(step > 0)
        def _():
            a2a_copy(d).wait()

        cross_copy(d).wait()
        rows = jnp.concatenate([ph_all[0, a], ph_all[1, a]], axis=0)
        mirrored = [
            jnp.dot(rows[:, b : b + LANES], flip, preferred_element_type=F32)
            for b in range(0, n_cols, LANES)
        ]
        both = jnp.concatenate(
            [rows.astype(F32), jnp.concatenate(mirrored[::-1], axis=1)], axis=0
        )
        lhs[:64, :] = both.astype(BF16)
        lhs[64:, :] = pltpu.roll(both, n_cols - 1, 1).astype(BF16)

        @pl.loop(0, n_rows // 16)
        def _(group):
            for pair in range(8):
                project(a, group * 8 + pair)

        @pl.when(step == n_angle - 2)
        def _():
            gather_probe()

    n_groups = n_rows // 8
    group_cols = 8 * LANES

    def group_at(owner, group, side):
        row = owner * n_rows + group * 8
        if side:
            row = NG - row - 8
        return pl.ds(pl.multiple_of(row * LANES, LANES), group_cols)

    def part_copy(group, side):
        at = vol.at[1 - core_at, :, group_at(core_at, group, side)]
        return remote(at, at, part_s.at[group, side], part_r.at[group, side], strip=mate)

    def part_arrived(group, side):
        at = vol.at[core_at, :, group_at(1 - core_at, group, side)]
        return remote(at, at, part_s.at[group, side], part_r.at[group, side], strip=mate)

    def store_part(owner, group, side, sem):
        cols = group_at(owner, group, side)
        return pltpu.make_async_copy(vol.at[core_at, :, cols], vol_hbm.at[:, cols], sem)

    @pl.loop(0, n_groups)
    def _(group):
        stack = jnp.concatenate([total[group * 8 + k, 32:] for k in range(8)], axis=0)
        turned = joined(jnp.dot(split(stack), flip, preferred_element_type=F32))
        for k in range(8):
            x = first_row + group * 8 + k
            here = pl.ds(pl.multiple_of(x * LANES, LANES), LANES)
            there = pl.ds(pl.multiple_of((NG - 1 - x) * LANES, LANES), LANES)
            for c in range(2):
                vol[c, :, here] = total[group * 8 + k, c * 16 : c * 16 + 16]
                vol[c, :, there] = turned[k * 32 + c * 16 : k * 32 + c * 16 + 16]
        for side in range(2):
            part_copy(group, side).start()
            store_part(core_at, group, side, own_sem.at[group, side]).start()

    def ag_arrived(d):
        sender = lax.rem(me_s + n_strip - d, n_strip)
        rows = pl.ds(pl.multiple_of(sender * 16, 16), 16)
        return remote(ag_in.at[rows], ag_in.at[rows], ag_s.at[d], ag_r.at[d], strip=sender)

    @pl.loop(1, n_strip)
    def _(d):
        ag_copy(d).wait_send()
        ag_arrived(d).wait_recv()

    pg_out[...] = ag_in[...].astype(F32)
    store_pg = pltpu.make_async_copy(pg_out, pg_hbm, store_sem.at[2])
    store_pg.start()
    @pl.loop(0, n_groups)
    def _(group):
        for side in range(2):
            part_arrived(group, side).wait_recv()
            store_part(1 - core_at, group, side, mate_sem.at[group, side]).start()

    @pl.loop(0, n_groups)
    def _(group):
        for side in range(2):
            part_copy(group, side).wait_send()
            store_part(core_at, group, side, own_sem.at[group, side]).wait()
            store_part(1 - core_at, group, side, mate_sem.at[group, side]).wait()

    store_og.wait()
    store_pg.wait()


def shards(object_field, amplitudes, scan_offsets, probe_field, tilt_angles):
    n_angle, n_strip = lax.axis_size("angle"), lax.axis_size("strip")
    width = object_field.shape[3]
    fwd, inv = dft_blocks()
    trig = jnp.stack([jnp.cos(tilt_angles), jnp.sin(tilt_angles)])
    scale = 1.0 / math.sqrt(n_angle * n_strip * scan_offsets.shape[1])
    n_cols = WINDOW[1] - WINDOW[0]
    parts = (NG // 32, 2)
    hbm = pl.BlockSpec(memory_space=pltpu.HBM)
    smem = pl.BlockSpec(memory_space=pltpu.SMEM)
    vmem, dma = pltpu.VMEM, pltpu.SemaphoreType.DMA
    object_grad, probe_grad, volume = pl.pallas_call(
        lambda *refs: kernel(n_angle, n_strip, scale, *refs),
        out_shape=(
            jax.ShapeDtypeStruct((2, 128, width), F32),
            jax.ShapeDtypeStruct((2 * FRAME, FRAME), F32),
            jax.ShapeDtypeStruct((16, NG * NG), F32),
        ),
        in_specs=[smem, smem] + [hbm] * 5,
        out_specs=(hbm, hbm, hbm),
        scratch_shapes=[
            vmem((2, FRAME, width), F32),
            vmem((2, FRAME, FRAME), F32),
            vmem((4, FRAME, FRAME), BF16),
            vmem((2 * FRAME, 2 * FRAME), BF16),
            vmem((2 * FRAME, 2 * FRAME), BF16),
            vmem((2, 2, HALO, width), BF16),
            vmem((2, 2, HALO, width), BF16),
            vmem((width, FRAME), BF16),
            vmem((FRAME, width), BF16),
            vmem((2, HALO, width), F32),
            vmem((2, FRAME, FRAME), F32),
            vmem((4, 4 * HALO, 2 * FRAME), BF16),
            vmem((4, 2 * FRAME, FRAME), BF16),
            vmem((4, 2 * FRAME, FRAME), F32),
            vmem((4, 2 * FRAME, FRAME), BF16),
            vmem((4, 4 * HALO, 2 * FRAME), BF16),
            vmem((4 * HALO, 2 * FRAME), F32),
            vmem((2, 2, HALO, width), BF16),
            vmem((2, 2, HALO, width), BF16),
            vmem((2, 128, width), F32),
            vmem((128, n_cols), BF16),
            vmem((2, n_angle, 16, n_cols), BF16),
            vmem((2 * FRAME, FRAME), BF16),
            vmem((n_strip, 16, FRAME), BF16),
            vmem((n_angle, 16, FRAME), BF16),
            vmem((2 * FRAME, FRAME), BF16),
            vmem((2 * FRAME, FRAME), F32),
            vmem((n_angle, NG // 4, LANES), F32),
            vmem((n_angle, NG // 4, LANES), F32),
            vmem((128, n_cols), BF16),
            vmem((NG // 4, 64, LANES), F32),
            vmem((2, 16, NG * NG), F32),
            dma((5,)), dma((3,)), dma((2,)), dma((2,)), dma((2,)), dma((2,)),
            dma((n_angle,)), dma((n_angle,)), dma((n_strip,)), dma((n_strip,)),
            dma((n_angle,)), dma((n_angle,)), dma((n_strip,)), dma((n_strip,)),
            dma((n_angle,)), dma((n_angle,)), dma(parts), dma(parts), dma(parts), dma(parts),
        ],
        compiler_params=pltpu.CompilerParams(
            collective_id=0, has_side_effects=True, vmem_limit_bytes=60 * 1024 * 1024
        ),
        name="gradient_step",
    )(
        scan_offsets.transpose(0, 2, 1), trig, object_field[:, 0], amplitudes[0], probe_field, fwd, inv
    )
    return (
        object_grad[:, None],
        probe_grad.reshape(2, FRAME, FRAME),
        volume[None, None],
    )


def solution(mesh):
    return jax.shard_map(
        shards,
        mesh=mesh,
        in_specs=(
            P(None, "angle", "strip", None),
            P("angle", "strip", None, None),
            P("angle", "strip", None),
            P(),
            P(),
        ),
        out_specs=(P(None, "angle", "strip", None), P(), P("strip", "angle", None, None)),
        check_vma=False,
    )
```

```python
import math

import jax
import jax.numpy as jnp
import numpy as np
from jax import lax
from jax.experimental import pallas as pl
from jax.experimental.pallas import tpu as pltpu
from jax.sharding import PartitionSpec as P

FRAME = 256
HALO = 64
NG = 128
LANES = 128
MESH = pl.DeviceIdType.MESH
F32 = jnp.float32
BF16 = jnp.bfloat16
FIXED_COLS = (768, 0, 384)
WINDOW = (320, 704)


def dft_blocks():
    index = np.arange(FRAME)
    angle = 2.0 * np.pi / FRAME * ((index[:, None] * index[None, :]) % FRAME)
    cos_tab = np.cos(angle) / math.sqrt(FRAME)
    sin_tab = np.sin(angle) / math.sqrt(FRAME)
    fwd = np.block([[cos_tab, sin_tab], [-sin_tab, cos_tab]])
    inv = np.block([[cos_tab, -sin_tab], [sin_tab, cos_tab]])
    return jnp.asarray(fwd, BF16), jnp.asarray(inv, BF16)


def kernel(
    n_angle, n_strip, scale,
    offs, trig, obj_hbm, amp_hbm, probe_hbm, fwd_hbm, inv_hbm,
    og_hbm, pg_hbm, vol_hbm,
    ext, probe, amp, fwd, inv,
    halo_out, halo_in, place_t, place_m, moved3, patch3, xbuf, ybuf, wbuf, mbuf, zbuf, gbuf,
    grad_out, grad_in, core, phase, ph_all,
    pterm, rs_in, ar_in, ag_in, pg_out,
    lower_t, frac_t, lhs, total, vol, vol_in,
    load_sem, store_sem, halo_s, halo_r, grad_s, grad_r, a2a_s, a2a_r,
    rs_s, rs_r, ar_s, ar_r, ag_s, ag_r, part_s, part_r, own_sem,
):
    width = ext.shape[2]
    me_a = lax.axis_index("angle")
    me_s = lax.axis_index("strip")
    above = lax.rem(me_s + n_strip - 1, n_strip)
    below = lax.rem(me_s + 1, n_strip)
    core_at = lax.rem(me_s, 2)
    mate = me_s + 1 - 2 * core_at

    loads = [
        pltpu.make_async_copy(obj_hbm, ext.at[:, pl.ds(HALO, 128), :], load_sem.at[0]),
        pltpu.make_async_copy(probe_hbm, probe, load_sem.at[1]),
        pltpu.make_async_copy(inv_hbm, inv, load_sem.at[2]),
        pltpu.make_async_copy(fwd_hbm, fwd, load_sem.at[3]),
        pltpu.make_async_copy(amp_hbm, amp, load_sem.at[4]),
    ]
    for load in loads:
        load.start()

    barrier = pltpu.get_barrier_semaphore()

    @pl.loop(1, n_strip)
    def _(d):
        pl.semaphore_signal(
            barrier, inc=1, device_id={"strip": lax.rem(me_s + d, n_strip)}, device_id_type=MESH
        )

    @pl.loop(1, n_angle)
    def _(d):
        pl.semaphore_signal(
            barrier, inc=1, device_id={"angle": lax.rem(me_a + d, n_angle)}, device_id_type=MESH
        )

    def phase_sender(side, kind):
        strip_to = me_s - core_at + side
        if kind == 0:
            return strip_to
        neighbour = jnp.where(me_a >= n_angle // 2, strip_to + 1, strip_to + n_strip - 1)
        return lax.rem(neighbour, n_strip)

    def phase_target(kind, peer):
        if kind == 0:
            row, strip_to = HALO + peer * 16, me_s
        else:
            upper = peer >= n_angle // 2
            row = jnp.where(upper, (peer - n_angle // 2) * 16, 3 * HALO + peer * 16)
            strip_to = jnp.where(upper, above, below)
        side = lax.rem(strip_to, 2)
        return row, side, strip_to - side + lax.rem(me_a, 2)

    @pl.loop(0, n_angle // 2)
    def _(g):
        a = 2 * g + core_at
        for side in range(2):
            for kind in range(2):
                sender = phase_sender(side, kind)

                @pl.when(jnp.logical_or(a != me_a, sender != me_s))
                def _():
                    pl.semaphore_signal(
                        barrier, inc=1, device_id={"angle": a, "strip": sender}, device_id_type=MESH
                    )

    messages = 2 * n_angle
    for kind in range(2):
        messages = messages - jnp.where(phase_target(kind, me_a)[2] == me_s, 1, 0)

    loads[0].wait()
    for side, first in ((0, HALO), (1, 2 * HALO)):

        @pl.loop(0, 4)
        def _(step):
            rows = pl.multiple_of(step * 16, 16)
            for part in range(2):
                halo_out[side, part, pl.ds(rows, 16), :] = ext[
                    part, pl.ds(first + rows, 16), :
                ].astype(BF16)

    pl.semaphore_wait(barrier, n_strip - 1 + n_angle - 1 + messages)

    def remote(src, dst, send, recv, **where):
        return pltpu.make_async_remote_copy(
            src_ref=src, dst_ref=dst, send_sem=send, recv_sem=recv,
            device_id=where, device_id_type=MESH,
        )

    halo_copies = [
        remote(halo_out.at[1], halo_in.at[0], halo_s.at[0], halo_r.at[0], strip=below),
        remote(halo_out.at[0], halo_in.at[1], halo_s.at[1], halo_r.at[1], strip=above),
    ]
    for copy in halo_copies:
        copy.start()

    col = offs[0, 1, 3].astype(F32)
    for b in range(width // LANES):
        at = lax.broadcasted_iota(jnp.int32, (LANES, FRAME), 0) + b * LANES
        of = lax.broadcasted_iota(jnp.int32, (LANES, FRAME), 1)
        place_t[b * LANES : (b + 1) * LANES, :] = ((at - of).astype(F32) == col).astype(F32).astype(BF16)
        at = lax.broadcasted_iota(jnp.int32, (FRAME, LANES), 1) + b * LANES
        of = lax.broadcasted_iota(jnp.int32, (FRAME, LANES), 0)
        place_m[:, b * LANES : (b + 1) * LANES] = ((at - of).astype(F32) == col).astype(F32).astype(BF16)

    def split(value):
        high = value.astype(BF16)
        return jnp.concatenate([high, (value - high.astype(F32)).astype(BF16)], axis=0)

    def joined(product):
        rows = product.shape[0] // 2
        return product[:rows] + product[rows:]

    def exit_chunk(chunk):
        rows = pl.ds(chunk * HALO, HALO)
        for part in range(2):
            patch3[part, rows, :] = joined(
                jnp.dot(split(ext[part, rows, :]), place_t[...], preferred_element_type=F32)
            )

        @pl.loop(0, 4)
        def _(step):
            local = pl.multiple_of(step * 16, 16)
            row = chunk * HALO + local
            pr, pi = probe[0, pl.ds(row, 16), :], probe[1, pl.ds(row, 16), :]
            res, ims = [
                [ext[part, pl.ds(row, 16), c : c + FRAME] for c in FIXED_COLS]
                + [patch3[part, pl.ds(row, 16), :]]
                for part in range(2)
            ]
            for f in range(4):
                xbuf[chunk, pl.ds(f * HALO + local, 16), :FRAME] = (
                    pr * res[f] - pi * ims[f]
                ).astype(BF16)
                xbuf[chunk, pl.ds(f * HALO + local, 16), FRAME:] = (
                    pr * ims[f] + pi * res[f]
                ).astype(BF16)

        half = jnp.dot(xbuf[chunk], inv[...], preferred_element_type=F32).astype(BF16)
        for f in range(4):
            at = f * HALO
            ybuf[f, pl.ds(chunk * HALO, HALO), :] = half[at : at + HALO, :FRAME]
            ybuf[f, pl.ds(FRAME + chunk * HALO, HALO), :] = half[at : at + HALO, FRAME:]

    loads[1].wait()
    loads[2].wait()
    exit_chunk(1)
    exit_chunk(2)

    center = (NG - 1) / 2.0
    n_rows = NG // 2
    shape = (n_rows, LANES)
    xpos = lax.broadcasted_iota(jnp.int32, shape, 0).astype(F32) - center
    ypos = lax.broadcasted_iota(jnp.int32, shape, 1).astype(F32) - center
    n_turns = n_angle // 2

    @pl.loop(0, n_turns)
    def _(g):
        a = 2 * g + core_at
        upos = (width - 1) / 2.0 + 2.0 * (xpos * trig[0, a] + ypos * trig[1, a])
        low = jnp.clip(jnp.floor(upos), 0.0, width - 2.0)
        lower_t[g] = low - float(WINDOW[0])
        frac_t[g] = upos - low
        each = n_rows // n_turns
        total[pl.ds(g * each, each)] = jnp.zeros((each, 64, LANES), F32)

    for copy in halo_copies:
        copy.wait()
    has_above = (me_s > 0).astype(F32)
    has_below = (me_s < n_strip - 1).astype(F32)
    for side, first, present in ((0, 0, has_above), (1, 3 * HALO, has_below)):

        @pl.loop(0, 4)
        def _(step):
            rows = pl.multiple_of(step * 16, 16)
            for part in range(2):
                ext[part, pl.ds(first + rows, 16), :] = (
                    halo_in[side, part, pl.ds(rows, 16), :].astype(F32) * present
                )

    exit_chunk(0)
    exit_chunk(3)

    loads[3].wait()
    loads[4].wait()

    def misfit(f, rows):
        wr, wi = wbuf[f, rows, :], wbuf[f, rows.start + FRAME : rows.stop + FRAME, :]
        measured = amp[f, rows, :].astype(F32)
        factor = 1.0 - measured * lax.rsqrt(wr * wr + wi * wi + 1.0)
        mbuf[f, rows, :] = (wr * factor).astype(BF16)
        mbuf[f, rows.start + FRAME : rows.stop + FRAME, :] = (wi * factor).astype(BF16)

    for f in range(4):
        wbuf[f] = jnp.dot(fwd[...], ybuf[f], preferred_element_type=F32)
        for row in range(0, FRAME, 32):
            misfit(f, slice(row, row + 32))
    for f in range(4):
        back = jnp.dot(inv[...], mbuf[f], preferred_element_type=F32).astype(BF16)
        for chunk in range(4):
            at = chunk * HALO
            zbuf[chunk, f * HALO : (f + 1) * HALO, :FRAME] = back[at : at + HALO]
            zbuf[chunk, f * HALO : (f + 1) * HALO, FRAME:] = back[FRAME + at : FRAME + at + HALO]

    def place(terms, moved):
        blocks = [moved[:, b * LANES : (b + 1) * LANES] for b in range(width // LANES)]
        for f in range(3):
            b = FIXED_COLS[f] // LANES
            blocks[b] = blocks[b] + terms[f][:, :LANES]
            blocks[b + 1] = blocks[b + 1] + terms[f][:, LANES:]
        return blocks

    around = (WINDOW[0] // LANES * LANES, -(-WINDOW[1] // LANES) * LANES)

    def grad_chunk(chunk):
        gbuf[...] = jnp.dot(zbuf[chunk], fwd[...], preferred_element_type=F32)
        rows = pl.ds(chunk * HALO, HALO)
        pr, pi = probe[0, rows, :], probe[1, rows, :]
        gr, gi = gbuf[3 * HALO :, :FRAME], gbuf[3 * HALO :, FRAME:]
        for part, value in ((0, pr * gr + pi * gi), (1, pr * gi - pi * gr)):
            moved3[part] = joined(
                jnp.dot(split(value), place_m[...], preferred_element_type=F32)
            )

        @pl.loop(0, 4)
        def _(step):
            local = pl.multiple_of(step * 16, 16)
            row = chunk * HALO + local
            rows = pl.ds(row, 16)
            pr, pi = probe[0, rows, :], probe[1, rows, :]
            t_re, t_im, q_re, q_im = [], [], 0.0, 0.0
            for f in range(4):
                gr = gbuf[pl.ds(f * HALO + local, 16), :FRAME]
                gi = gbuf[pl.ds(f * HALO + local, 16), FRAME:]
                if f < 3:
                    t_re.append(pr * gr + pi * gi)
                    t_im.append(pr * gi - pi * gr)
                    c = FIXED_COLS[f]
                    er, ei = ext[0, rows, c : c + FRAME], ext[1, rows, c : c + FRAME]
                else:
                    er, ei = patch3[0, rows, :], patch3[1, rows, :]
                q_re = q_re + (er * gr + ei * gi)
                q_im = q_im + (er * gi - ei * gr)
            pterm[pl.ds(row, 16), :] = q_re.astype(BF16)
            pterm[pl.ds(FRAME + row, 16), :] = q_im.astype(BF16)
            sums = [
                place(terms, moved3[part, pl.ds(local, 16), :])
                for part, terms in ((0, t_re), (1, t_im))
            ]
            for part in range(2):
                for b, value in enumerate(sums[part]):
                    cols = slice(b * LANES, (b + 1) * LANES)
                    if chunk in (0, 3):
                        grad_out[chunk // 3, part, pl.ds(local, 16), cols] = value.astype(BF16)
                    else:
                        core[part, pl.ds((chunk - 1) * HALO + local, 16), cols] = value
            value = jnp.concatenate(
                [
                    ext[0, rows, b * LANES : (b + 1) * LANES] * sums[1][b]
                    - ext[1, rows, b * LANES : (b + 1) * LANES] * sums[0][b]
                    for b in range(around[0] // LANES, around[1] // LANES)
                ],
                axis=1,
            )
            value = pltpu.roll(value, around[1] - WINDOW[0], 1)
            phase[rows, :] = value[:, : WINDOW[1] - WINDOW[0]].astype(BF16)

    def phase_copy(kind, peer):
        row, side, to = phase_target(kind, peer)
        src = phase.at[pl.ds(pl.multiple_of(row, 16), 16)]
        dst = ph_all.at[me_a // 2, side, kind]
        copy = remote(
            src, dst, a2a_s.at[kind, peer], a2a_r.at[me_a // 2, side, kind], angle=peer, strip=to
        )
        stays = jnp.logical_and(peer == me_a, to == me_s)
        return copy, stays, src, dst

    def send_phase(kind, first):
        @pl.loop(first, first + n_angle // 2)
        def _(peer):
            copy, stays, src, dst = phase_copy(kind, peer)

            @pl.when(stays)
            def _():
                dst[...] = src[...]

            @pl.when(jnp.logical_not(stays))
            def _():
                copy.start()

    grad_chunk(0)
    send_phase(1, n_angle // 2)
    grad_chunk(3)
    send_phase(1, 0)
    grad_chunk(1)
    send_phase(0, 0)
    grad_chunk(2)
    send_phase(0, n_angle // 2)

    def rs_copy(d):
        peer = lax.rem(me_s + d, n_strip)
        return remote(
            pterm.at[pl.ds(pl.multiple_of(peer * 16, 16), 16)], rs_in.at[d],
            rs_s.at[d], rs_r.at[d], strip=peer,
        )

    @pl.loop(1, n_strip)
    def _(d):
        rs_copy(d).start()

    grad_copies = [
        remote(grad_out.at[1], grad_in.at[0], grad_s.at[0], grad_r.at[0], strip=below),
        remote(grad_out.at[0], grad_in.at[1], grad_s.at[1], grad_r.at[1], strip=above),
    ]
    for copy in grad_copies:
        copy.start()

    own_rows = pl.ds(pl.multiple_of(me_s * 16, 16), 16)

    def ar_copy(d):
        peer = lax.rem(me_a + d, n_angle)
        return remote(
            ar_in.at[me_a], ar_in.at[me_a], ar_s.at[d], ar_r.at[d], angle=peer
        )

    store_og = pltpu.make_async_copy(core, og_hbm, store_sem.at[0])

    def finish_object():
        for copy in grad_copies:
            copy.wait()
        for side, present in ((0, has_above), (1, has_below)):

            @pl.loop(0, 4)
            def _(step):
                local = pl.multiple_of(step * 16, 16)
                rows = pl.ds(side * HALO + local, 16)
                for part in range(2):
                    core[part, rows, :] += (
                        grad_in[side, part, pl.ds(local, 16), :].astype(F32) * present
                    )

        store_og.start()

    def exchange_probe():
        @pl.loop(1, n_strip)
        def _(d):
            rs_copy(d).wait()

        ar_in[me_a] = lax.fori_loop(
            1, n_strip, lambda d, acc: acc + rs_in[d].astype(F32), pterm[own_rows, :].astype(F32)
        ).astype(BF16)

        @pl.loop(1, n_angle)
        def _(d):
            ar_copy(d).start()

    flip = (
        lax.broadcasted_iota(jnp.int32, (LANES, LANES), 0)
        + lax.broadcasted_iota(jnp.int32, (LANES, LANES), 1)
        == LANES - 1
    ).astype(F32).astype(BF16)
    n_cols = WINDOW[1] - WINDOW[0]
    column = lax.broadcasted_iota(jnp.int32, (LANES, LANES), 0).astype(F32).astype(BF16)
    one, zero = jnp.ones((), BF16), jnp.zeros((), BF16)

    def ag_copy(d):
        peer = lax.rem(me_s + d, n_strip)
        return remote(
            ag_in.at[own_rows], ag_in.at[own_rows], ag_s.at[d], ag_r.at[d], strip=peer
        )

    def gather_probe():
        @pl.loop(1, n_angle)
        def _(d):
            ar_copy(d).wait()

        summed = ar_in[0].astype(F32)
        for a in range(1, n_angle):
            summed = summed + ar_in[a].astype(F32)
        ag_in[own_rows, :] = (summed * scale).astype(BF16)

        @pl.loop(1, n_strip)
        def _(d):
            ag_copy(d).start()

    def one_hot(g, i):
        low = lower_t[g, pl.ds(i, 1), :]
        return jnp.concatenate(
            [
                jnp.where(column == (low - float(j)).astype(BF16), one, zero)
                for j in range(0, n_cols, LANES)
            ],
            axis=0,
        )

    def project(g, pair):
        picks = jnp.concatenate([one_hot(g, 2 * pair + k) for k in range(2)], axis=1)
        got = jnp.dot(lhs[...], picks, preferred_element_type=F32)
        for k in range(2):
            frac = frac_t[g, pl.ds(2 * pair + k, 1), :]
            part = got[:, k * LANES : (k + 1) * LANES]
            total[2 * pair + k] += part[:64] * (1.0 - frac) + part[64:] * frac

    n_groups = n_rows // 16
    group_cols = 16 * LANES

    def group_at(group, side):
        row = group * 16
        if side:
            row = NG - row - 16
        return pl.ds(pl.multiple_of(row * LANES, LANES), group_cols)

    def part_copy(group, side):
        cols = group_at(group, side)
        return remote(
            vol.at[1 - core_at, :, cols], vol_in.at[:, cols],
            part_s.at[group, side], part_r.at[group, side], strip=mate,
        )

    def store_part(group, side):
        cols = group_at(group, side)
        return pltpu.make_async_copy(
            vol.at[core_at, :, cols], vol_hbm.at[:, cols], own_sem.at[group, side]
        )

    def finish_group(group):
        stack = jnp.concatenate([total[group * 16 + k, 32:] for k in range(16)], axis=0)
        turned = joined(jnp.dot(split(stack), flip, preferred_element_type=F32))
        for k in range(16):
            x = group * 16 + k
            here = pl.ds(pl.multiple_of(x * LANES, LANES), LANES)
            there = pl.ds(pl.multiple_of((NG - 1 - x) * LANES, LANES), LANES)
            for c in range(2):
                vol[c, :, here] = total[x, c * 16 : c * 16 + 16]
                vol[c, :, there] = turned[k * 32 + c * 16 : k * 32 + c * 16 + 16]
        for side in range(2):
            part_copy(group, side).start()

    same = lax.rem(me_a + core_at, 2) == 0

    @pl.loop(0, n_turns)
    def _(step):
        odd = lax.rem(step, 2)
        even_far = jnp.where(odd == 1, step + 1, n_angle - step)
        odd_far = jnp.where(odd == 1, n_angle - step, step + 1)
        a = lax.rem(me_a + jnp.where(same, even_far, odd_far), n_angle)
        g = a // 2
        for side in range(2):
            for kind in range(2):
                sender = phase_sender(side, kind)
                dst = ph_all.at[g, side, kind]

                @pl.when(jnp.logical_or(a != me_a, sender != me_s))
                def _():
                    remote(
                        dst, dst, a2a_s.at[kind, 0], a2a_r.at[g, side, kind], strip=mate
                    ).wait_recv()

        rows = jnp.concatenate(
            [ph_all[g, side, 0].astype(F32) + ph_all[g, side, 1].astype(F32) for side in range(2)],
            axis=0,
        ).astype(BF16)
        mirrored = [
            jnp.dot(rows[:, b : b + LANES], flip, preferred_element_type=F32)
            for b in range(0, n_cols, LANES)
        ]
        both = jnp.concatenate(
            [rows.astype(F32), jnp.concatenate(mirrored[::-1], axis=1)], axis=0
        )
        lhs[:64, :] = both.astype(BF16)
        lhs[64:, :] = pltpu.roll(both, n_cols - 1, 1).astype(BF16)

        @pl.loop(0, n_groups)
        def _(group):
            for pair in range(8):
                project(g, group * 8 + pair)

            @pl.when(step == n_turns - 1)
            def _():
                finish_group(group)

        @pl.when(step == 0)
        def _():
            exchange_probe()

        @pl.when(step == 1)
        def _():
            finish_object()

        @pl.when(step == n_turns - 2)
        def _():
            gather_probe()

    @pl.loop(0, n_angle)
    def _(peer):
        for kind in range(2):
            copy, stays, _, _ = phase_copy(kind, peer)

            @pl.when(jnp.logical_not(stays))
            def _():
                copy.wait_send()

    @pl.loop(0, n_groups)
    def _(group):
        for side in range(2):
            part_copy(group, side).wait_recv()
            cols = group_at(group, side)
            vol[core_at, :, cols] += vol_in[:, cols]
            store_part(group, side).start()

    def ag_arrived(d):
        sender = lax.rem(me_s + n_strip - d, n_strip)
        rows = pl.ds(pl.multiple_of(sender * 16, 16), 16)
        return remote(ag_in.at[rows], ag_in.at[rows], ag_s.at[d], ag_r.at[d], strip=sender)

    @pl.loop(1, n_strip)
    def _(d):
        ag_copy(d).wait_send()
        ag_arrived(d).wait_recv()

    pg_out[...] = ag_in[...].astype(F32)
    store_pg = pltpu.make_async_copy(pg_out, pg_hbm, store_sem.at[2])
    store_pg.start()
    @pl.loop(0, n_groups)
    def _(group):
        for side in range(2):
            part_copy(group, side).wait_send()
            store_part(group, side).wait()

    store_og.wait()
    store_pg.wait()


def shards(object_field, amplitudes, scan_offsets, probe_field, tilt_angles):
    n_angle, n_strip = lax.axis_size("angle"), lax.axis_size("strip")
    width = object_field.shape[3]
    fwd, inv = dft_blocks()
    trig = jnp.stack([jnp.cos(tilt_angles), jnp.sin(tilt_angles)])
    scale = 1.0 / math.sqrt(n_angle * n_strip * scan_offsets.shape[1])
    n_cols = WINDOW[1] - WINDOW[0]
    parts = (NG // 32, 2)
    hbm = pl.BlockSpec(memory_space=pltpu.HBM)
    smem = pl.BlockSpec(memory_space=pltpu.SMEM)
    vmem, dma = pltpu.VMEM, pltpu.SemaphoreType.DMA
    object_grad, probe_grad, volume = pl.pallas_call(
        lambda *refs: kernel(n_angle, n_strip, scale, *refs),
        out_shape=(
            jax.ShapeDtypeStruct((2, 128, width), F32),
            jax.ShapeDtypeStruct((2 * FRAME, FRAME), F32),
            jax.ShapeDtypeStruct((16, NG * NG), F32),
        ),
        in_specs=[smem, smem] + [hbm] * 5,
        out_specs=(hbm, hbm, hbm),
        scratch_shapes=[
            vmem((2, FRAME, width), F32),
            vmem((2, FRAME, FRAME), F32),
            vmem((4, FRAME, FRAME), BF16),
            vmem((2 * FRAME, 2 * FRAME), BF16),
            vmem((2 * FRAME, 2 * FRAME), BF16),
            vmem((2, 2, HALO, width), BF16),
            vmem((2, 2, HALO, width), BF16),
            vmem((width, FRAME), BF16),
            vmem((FRAME, width), BF16),
            vmem((2, HALO, width), F32),
            vmem((2, FRAME, FRAME), F32),
            vmem((4, 4 * HALO, 2 * FRAME), BF16),
            vmem((4, 2 * FRAME, FRAME), BF16),
            vmem((4, 2 * FRAME, FRAME), F32),
            vmem((4, 2 * FRAME, FRAME), BF16),
            vmem((4, 4 * HALO, 2 * FRAME), BF16),
            vmem((4 * HALO, 2 * FRAME), F32),
            vmem((2, 2, HALO, width), BF16),
            vmem((2, 2, HALO, width), BF16),
            vmem((2, 128, width), F32),
            vmem((FRAME, n_cols), BF16),
            vmem((n_angle // 2, 2, 2, 16, n_cols), BF16),
            vmem((2 * FRAME, FRAME), BF16),
            vmem((n_strip, 16, FRAME), BF16),
            vmem((n_angle, 16, FRAME), BF16),
            vmem((2 * FRAME, FRAME), BF16),
            vmem((2 * FRAME, FRAME), F32),
            vmem((n_angle // 2, NG // 2, LANES), F32),
            vmem((n_angle // 2, NG // 2, LANES), F32),
            vmem((128, n_cols), BF16),
            vmem((NG // 2, 64, LANES), F32),
            vmem((2, 16, NG * NG), F32),
            vmem((16, NG * NG), F32),
            dma((5,)), dma((3,)), dma((2,)), dma((2,)), dma((2,)), dma((2,)),
            dma((2, n_angle)), dma((n_angle // 2, 2, 2)), dma((n_strip,)), dma((n_strip,)),
            dma((n_angle,)), dma((n_angle,)), dma((n_strip,)), dma((n_strip,)),
            dma(parts), dma(parts), dma(parts),
        ],
        compiler_params=pltpu.CompilerParams(
            collective_id=0, has_side_effects=True, vmem_limit_bytes=60 * 1024 * 1024
        ),
        name="gradient_step",
    )(
        scan_offsets.transpose(0, 2, 1), trig, object_field[:, 0], amplitudes[0], probe_field, fwd, inv
    )
    return (
        object_grad[:, None],
        probe_grad.reshape(2, FRAME, FRAME),
        volume[None, None],
    )


def solution(mesh):
    return jax.shard_map(
        shards,
        mesh=mesh,
        in_specs=(
            P(None, "angle", "strip", None),
            P("angle", "strip", None, None),
            P("angle", "strip", None),
            P(),
            P(),
        ),
        out_specs=(P(None, "angle", "strip", None), P(), P("strip", "angle", None, None)),
        check_vma=False,
    )
```

```python
import math

import jax
import jax.numpy as jnp
import numpy as np
from jax import lax
from jax.experimental import pallas as pl
from jax.experimental.pallas import tpu as pltpu
from jax.sharding import PartitionSpec as P

FRAME = 256
HALO = 64
NG = 128
LANES = 128
MESH = pl.DeviceIdType.MESH
F32 = jnp.float32
BF16 = jnp.bfloat16
FIXED_COLS = (768, 0, 384)
WINDOW = (320, 704)


def dft_blocks():
    index = np.arange(FRAME)
    angle = 2.0 * np.pi / FRAME * ((index[:, None] * index[None, :]) % FRAME)
    cos_tab = np.cos(angle) / math.sqrt(FRAME)
    sin_tab = np.sin(angle) / math.sqrt(FRAME)
    fwd = np.block([[cos_tab, sin_tab], [-sin_tab, cos_tab]])
    inv = np.block([[cos_tab, -sin_tab], [sin_tab, cos_tab]])
    return jnp.asarray(fwd, BF16), jnp.asarray(inv, BF16)


def kernel(
    n_angle, n_strip, scale,
    offs, trig, obj_hbm, amp_hbm, probe_hbm, fwd_hbm, inv_hbm,
    og_hbm, pg_hbm, vol_hbm,
    ext, probe, amp, fwd, inv,
    halo_out, halo_in, place_t, place_m, moved3, patch3, xbuf, ybuf, wbuf, mbuf, zbuf, gbuf,
    grad_out, grad_in, core, phase, ph_all,
    pterm, rs_in, ar_in, ag_in, pg_out,
    lower_t, frac_t, lhs, total, vol, vol_in,
    load_sem, store_sem, halo_s, halo_r, grad_s, grad_r, a2a_s, a2a_r,
    rs_s, rs_r, ar_s, ar_r, ag_s, ag_r, part_s, part_r, own_sem,
):
    width = ext.shape[2]
    me_a = lax.axis_index("angle")
    me_s = lax.axis_index("strip")
    above = lax.rem(me_s + n_strip - 1, n_strip)
    below = lax.rem(me_s + 1, n_strip)
    core_at = lax.rem(me_s, 2)
    mate = me_s + 1 - 2 * core_at

    loads = [
        pltpu.make_async_copy(obj_hbm, ext.at[:, pl.ds(HALO, 128), :], load_sem.at[0]),
        pltpu.make_async_copy(probe_hbm, probe, load_sem.at[1]),
        pltpu.make_async_copy(inv_hbm, inv, load_sem.at[2]),
        pltpu.make_async_copy(fwd_hbm, fwd, load_sem.at[3]),
        pltpu.make_async_copy(amp_hbm, amp, load_sem.at[4]),
    ]
    for load in loads:
        load.start()

    barrier = pltpu.get_barrier_semaphore()

    pl.semaphore_signal(barrier, inc=1, device_id={"strip": above}, device_id_type=MESH)

    @pl.loop(1, n_strip - 1)
    def _(d):
        pl.semaphore_signal(
            barrier, inc=1, device_id={"strip": lax.rem(me_s + d, n_strip)}, device_id_type=MESH
        )

    @pl.loop(1, n_angle)
    def _(d):
        pl.semaphore_signal(
            barrier, inc=1, device_id={"angle": lax.rem(me_a + d, n_angle)}, device_id_type=MESH
        )

    def phase_sender(side, kind):
        strip_to = me_s - core_at + side
        if kind == 0:
            return strip_to
        neighbour = jnp.where(me_a >= n_angle // 2, strip_to + 1, strip_to + n_strip - 1)
        return lax.rem(neighbour, n_strip)

    def phase_target(kind, peer):
        if kind == 0:
            row, strip_to = HALO + peer * 16, me_s
        else:
            upper = peer >= n_angle // 2
            row = jnp.where(upper, (peer - n_angle // 2) * 16, 3 * HALO + peer * 16)
            strip_to = jnp.where(upper, above, below)
        side = lax.rem(strip_to, 2)
        return row, side, strip_to - side + lax.rem(me_a, 2)

    @pl.loop(0, n_angle // 2)
    def _(g):
        a = 2 * g + core_at
        for side in range(2):
            for kind in range(2):
                sender = phase_sender(side, kind)

                @pl.when(jnp.logical_or(a != me_a, sender != me_s))
                def _():
                    pl.semaphore_signal(
                        barrier, inc=1, device_id={"angle": a, "strip": sender}, device_id_type=MESH
                    )

    messages = 2 * n_angle
    for kind in range(2):
        messages = messages - jnp.where(phase_target(kind, me_a)[2] == me_s, 1, 0)

    loads[0].wait()
    for side, first in ((0, HALO), (1, 2 * HALO)):

        @pl.loop(0, 4)
        def _(step):
            rows = pl.multiple_of(step * 16, 16)
            for part in range(2):
                halo_out[side, part, pl.ds(rows, 16), :] = ext[
                    part, pl.ds(first + rows, 16), :
                ].astype(BF16)

    pl.semaphore_wait(barrier, n_strip - 1 + n_angle - 1 + messages)

    def remote(src, dst, send, recv, **where):
        return pltpu.make_async_remote_copy(
            src_ref=src, dst_ref=dst, send_sem=send, recv_sem=recv,
            device_id=where, device_id_type=MESH,
        )

    halo_copies = [
        remote(halo_out.at[1], halo_in.at[0], halo_s.at[0], halo_r.at[0], strip=below),
        remote(halo_out.at[0], halo_in.at[1], halo_s.at[1], halo_r.at[1], strip=above),
    ]
    for copy in halo_copies:
        copy.start()

    col = offs[0, 1, 3].astype(F32)
    for b in range(width // LANES):
        at = lax.broadcasted_iota(jnp.int32, (LANES, FRAME), 0) + b * LANES
        of = lax.broadcasted_iota(jnp.int32, (LANES, FRAME), 1)
        place_t[b * LANES : (b + 1) * LANES, :] = ((at - of).astype(F32) == col).astype(F32).astype(BF16)
        at = lax.broadcasted_iota(jnp.int32, (FRAME, LANES), 1) + b * LANES
        of = lax.broadcasted_iota(jnp.int32, (FRAME, LANES), 0)
        place_m[:, b * LANES : (b + 1) * LANES] = ((at - of).astype(F32) == col).astype(F32).astype(BF16)

    def split(value):
        high = value.astype(BF16)
        return jnp.concatenate([high, (value - high.astype(F32)).astype(BF16)], axis=0)

    def joined(product):
        rows = product.shape[0] // 2
        return product[:rows] + product[rows:]

    def exit_chunk(chunk):
        rows = pl.ds(chunk * HALO, HALO)
        for part in range(2):
            patch3[part, rows, :] = joined(
                jnp.dot(split(ext[part, rows, :]), place_t[...], preferred_element_type=F32)
            )

        @pl.loop(0, 4)
        def _(step):
            local = pl.multiple_of(step * 16, 16)
            row = chunk * HALO + local
            pr, pi = probe[0, pl.ds(row, 16), :], probe[1, pl.ds(row, 16), :]
            res, ims = [
                [ext[part, pl.ds(row, 16), c : c + FRAME] for c in FIXED_COLS]
                + [patch3[part, pl.ds(row, 16), :]]
                for part in range(2)
            ]
            for f in range(4):
                xbuf[chunk, pl.ds(f * HALO + local, 16), :FRAME] = (
                    pr * res[f] - pi * ims[f]
                ).astype(BF16)
                xbuf[chunk, pl.ds(f * HALO + local, 16), FRAME:] = (
                    pr * ims[f] + pi * res[f]
                ).astype(BF16)

        half = jnp.dot(xbuf[chunk], inv[...], preferred_element_type=F32).astype(BF16)
        for f in range(4):
            at = f * HALO
            ybuf[f, pl.ds(chunk * HALO, HALO), :] = half[at : at + HALO, :FRAME]
            ybuf[f, pl.ds(FRAME + chunk * HALO, HALO), :] = half[at : at + HALO, FRAME:]

    loads[1].wait()
    loads[2].wait()
    exit_chunk(1)
    exit_chunk(2)

    center = (NG - 1) / 2.0
    n_rows = NG // 2
    shape = (n_rows, LANES)
    xpos = lax.broadcasted_iota(jnp.int32, shape, 0).astype(F32) - center
    ypos = lax.broadcasted_iota(jnp.int32, shape, 1).astype(F32) - center
    n_turns = n_angle // 2

    @pl.loop(0, n_turns)
    def _(g):
        a = 2 * g + core_at
        upos = (width - 1) / 2.0 + 2.0 * (xpos * trig[0, a] + ypos * trig[1, a])
        low = jnp.clip(jnp.floor(upos), 0.0, width - 2.0)
        lower_t[g] = low - float(WINDOW[0])
        frac_t[g] = upos - low
        each = n_rows // n_turns
        total[pl.ds(g * each, each)] = jnp.zeros((each, 64, LANES), F32)

    for copy in halo_copies:
        copy.wait()
    has_above = (me_s > 0).astype(F32)
    has_below = (me_s < n_strip - 1).astype(F32)
    for side, first, present in ((0, 0, has_above), (1, 3 * HALO, has_below)):

        @pl.loop(0, 4)
        def _(step):
            rows = pl.multiple_of(step * 16, 16)
            for part in range(2):
                ext[part, pl.ds(first + rows, 16), :] = (
                    halo_in[side, part, pl.ds(rows, 16), :].astype(F32) * present
                )

    exit_chunk(0)
    exit_chunk(3)

    loads[3].wait()
    loads[4].wait()

    def misfit(f, rows):
        wr, wi = wbuf[f, rows, :], wbuf[f, rows.start + FRAME : rows.stop + FRAME, :]
        measured = amp[f, rows, :].astype(F32)
        factor = 1.0 - measured * lax.rsqrt(wr * wr + wi * wi + 1.0)
        mbuf[f, rows, :] = (wr * factor).astype(BF16)
        mbuf[f, rows.start + FRAME : rows.stop + FRAME, :] = (wi * factor).astype(BF16)

    for f in range(4):
        wbuf[f] = jnp.dot(fwd[...], ybuf[f], preferred_element_type=F32)
        for row in range(0, FRAME, 32):
            misfit(f, slice(row, row + 32))
    for f in range(4):
        back = jnp.dot(inv[...], mbuf[f], preferred_element_type=F32).astype(BF16)
        for chunk in range(4):
            at = chunk * HALO
            zbuf[chunk, f * HALO : (f + 1) * HALO, :FRAME] = back[at : at + HALO]
            zbuf[chunk, f * HALO : (f + 1) * HALO, FRAME:] = back[FRAME + at : FRAME + at + HALO]

    def place(terms, moved):
        blocks = [moved[:, b * LANES : (b + 1) * LANES] for b in range(width // LANES)]
        for f in range(3):
            b = FIXED_COLS[f] // LANES
            blocks[b] = blocks[b] + terms[f][:, :LANES]
            blocks[b + 1] = blocks[b + 1] + terms[f][:, LANES:]
        return blocks

    around = (WINDOW[0] // LANES * LANES, -(-WINDOW[1] // LANES) * LANES)

    def grad_chunk(chunk):
        gbuf[...] = jnp.dot(zbuf[chunk], fwd[...], preferred_element_type=F32)
        rows = pl.ds(chunk * HALO, HALO)
        pr, pi = probe[0, rows, :], probe[1, rows, :]
        gr, gi = gbuf[3 * HALO :, :FRAME], gbuf[3 * HALO :, FRAME:]
        for part, value in ((0, pr * gr + pi * gi), (1, pr * gi - pi * gr)):
            moved3[part] = joined(
                jnp.dot(split(value), place_m[...], preferred_element_type=F32)
            )

        @pl.loop(0, 4)
        def _(step):
            local = pl.multiple_of(step * 16, 16)
            row = chunk * HALO + local
            rows = pl.ds(row, 16)
            pr, pi = probe[0, rows, :], probe[1, rows, :]
            t_re, t_im, q_re, q_im = [], [], 0.0, 0.0
            for f in range(4):
                gr = gbuf[pl.ds(f * HALO + local, 16), :FRAME]
                gi = gbuf[pl.ds(f * HALO + local, 16), FRAME:]
                if f < 3:
                    t_re.append(pr * gr + pi * gi)
                    t_im.append(pr * gi - pi * gr)
                    c = FIXED_COLS[f]
                    er, ei = ext[0, rows, c : c + FRAME], ext[1, rows, c : c + FRAME]
                else:
                    er, ei = patch3[0, rows, :], patch3[1, rows, :]
                q_re = q_re + (er * gr + ei * gi)
                q_im = q_im + (er * gi - ei * gr)
            pterm[pl.ds(row, 16), :] = q_re.astype(BF16)
            pterm[pl.ds(FRAME + row, 16), :] = q_im.astype(BF16)
            sums = [
                place(terms, moved3[part, pl.ds(local, 16), :])
                for part, terms in ((0, t_re), (1, t_im))
            ]
            for part in range(2):
                for b, value in enumerate(sums[part]):
                    cols = slice(b * LANES, (b + 1) * LANES)
                    if chunk in (0, 3):
                        grad_out[chunk // 3, part, pl.ds(local, 16), cols] = value.astype(BF16)
                    else:
                        core[part, pl.ds((chunk - 1) * HALO + local, 16), cols] = value
            value = jnp.concatenate(
                [
                    ext[0, rows, b * LANES : (b + 1) * LANES] * sums[1][b]
                    - ext[1, rows, b * LANES : (b + 1) * LANES] * sums[0][b]
                    for b in range(around[0] // LANES, around[1] // LANES)
                ],
                axis=1,
            )
            value = pltpu.roll(value, around[1] - WINDOW[0], 1)
            phase[rows, :] = value[:, : WINDOW[1] - WINDOW[0]].astype(BF16)

    def phase_copy(kind, peer):
        row, side, to = phase_target(kind, peer)
        src = phase.at[pl.ds(pl.multiple_of(row, 16), 16)]
        dst = ph_all.at[me_a // 2, side, kind]
        copy = remote(
            src, dst, a2a_s.at[kind, peer], a2a_r.at[me_a // 2, side, kind], angle=peer, strip=to
        )
        stays = jnp.logical_and(peer == me_a, to == me_s)
        return copy, stays, src, dst

    def send_phase(kind, first):
        @pl.loop(first, first + n_angle // 2)
        def _(peer):
            copy, stays, src, dst = phase_copy(kind, peer)

            @pl.when(stays)
            def _():
                dst[...] = src[...]

            @pl.when(jnp.logical_not(stays))
            def _():
                copy.start()

    grad_chunk(0)
    send_phase(1, n_angle // 2)
    grad_chunk(3)
    send_phase(1, 0)
    grad_chunk(1)
    send_phase(0, 0)
    grad_chunk(2)
    send_phase(0, n_angle // 2)

    def rs_copy(d):
        peer = lax.rem(me_s + d, n_strip)
        return remote(
            pterm.at[pl.ds(pl.multiple_of(peer * 16, 16), 16)], rs_in.at[d],
            rs_s.at[d], rs_r.at[d], strip=peer,
        )

    @pl.loop(1, n_strip)
    def _(d):
        rs_copy(d).start()

    grad_copies = [
        remote(grad_out.at[1], grad_in.at[0], grad_s.at[0], grad_r.at[0], strip=below),
        remote(grad_out.at[0], grad_in.at[1], grad_s.at[1], grad_r.at[1], strip=above),
    ]
    for copy in grad_copies:
        copy.start()

    own_rows = pl.ds(pl.multiple_of(me_s * 16, 16), 16)

    def ar_copy(d):
        peer = lax.rem(me_a + d, n_angle)
        return remote(
            ar_in.at[me_a], ar_in.at[me_a], ar_s.at[d], ar_r.at[d], angle=peer
        )

    store_og = pltpu.make_async_copy(core, og_hbm, store_sem.at[0])

    def finish_object():
        for copy in grad_copies:
            copy.wait()
        for side, present in ((0, has_above), (1, has_below)):

            @pl.loop(0, 4)
            def _(step):
                local = pl.multiple_of(step * 16, 16)
                rows = pl.ds(side * HALO + local, 16)
                for part in range(2):
                    core[part, rows, :] += (
                        grad_in[side, part, pl.ds(local, 16), :].astype(F32) * present
                    )

        store_og.start()

    def exchange_probe():
        @pl.loop(1, n_strip)
        def _(d):
            rs_copy(d).wait()

        ar_in[me_a] = lax.fori_loop(
            1, n_strip, lambda d, acc: acc + rs_in[d].astype(F32), pterm[own_rows, :].astype(F32)
        ).astype(BF16)

        @pl.loop(1, n_angle)
        def _(d):
            ar_copy(d).start()

    flip = (
        lax.broadcasted_iota(jnp.int32, (LANES, LANES), 0)
        + lax.broadcasted_iota(jnp.int32, (LANES, LANES), 1)
        == LANES - 1
    ).astype(F32).astype(BF16)
    n_cols = WINDOW[1] - WINDOW[0]
    column = lax.broadcasted_iota(jnp.int32, (LANES, LANES), 0).astype(F32).astype(BF16)
    one, zero = jnp.ones((), BF16), jnp.zeros((), BF16)

    def ag_copy(d):
        peer = lax.rem(me_s + d, n_strip)
        return remote(
            ag_in.at[own_rows], ag_in.at[own_rows], ag_s.at[d], ag_r.at[d], strip=peer
        )

    def gather_probe():
        @pl.loop(1, n_angle)
        def _(d):
            ar_copy(d).wait()

        summed = ar_in[0].astype(F32)
        for a in range(1, n_angle):
            summed = summed + ar_in[a].astype(F32)
        ag_in[own_rows, :] = (summed * scale).astype(BF16)

        @pl.loop(1, n_strip)
        def _(d):
            ag_copy(d).start()

    def one_hot(g, i):
        low = lower_t[g, pl.ds(i, 1), :]
        return jnp.concatenate(
            [
                jnp.where(column == (low - float(j)).astype(BF16), one, zero)
                for j in range(0, n_cols, LANES)
            ],
            axis=0,
        )

    def project(g, pair):
        picks = jnp.concatenate([one_hot(g, 2 * pair + k) for k in range(2)], axis=1)
        got = jnp.dot(lhs[...], picks, preferred_element_type=F32)
        for k in range(2):
            frac = frac_t[g, pl.ds(2 * pair + k, 1), :]
            part = got[:, k * LANES : (k + 1) * LANES]
            total[2 * pair + k] += part[:64] * (1.0 - frac) + part[64:] * frac

    n_groups = n_rows // 16
    group_cols = 16 * LANES

    def group_at(group, side):
        row = group * 16
        if side:
            row = NG - row - 16
        return pl.ds(pl.multiple_of(row * LANES, LANES), group_cols)

    def part_copy(group, side):
        cols = group_at(group, side)
        return remote(
            vol.at[1 - core_at, :, cols], vol_in.at[:, cols],
            part_s.at[group, side], part_r.at[group, side], strip=mate,
        )

    def store_part(group, side):
        cols = group_at(group, side)
        return pltpu.make_async_copy(
            vol.at[core_at, :, cols], vol_hbm.at[:, cols], own_sem.at[group, side]
        )

    def finish_group(group):
        stack = jnp.concatenate([total[group * 16 + k, 32:] for k in range(16)], axis=0)
        turned = joined(jnp.dot(split(stack), flip, preferred_element_type=F32))
        for k in range(16):
            x = group * 16 + k
            here = pl.ds(pl.multiple_of(x * LANES, LANES), LANES)
            there = pl.ds(pl.multiple_of((NG - 1 - x) * LANES, LANES), LANES)
            for c in range(2):
                vol[c, :, here] = total[x, c * 16 : c * 16 + 16]
                vol[c, :, there] = turned[k * 32 + c * 16 : k * 32 + c * 16 + 16]
        for side in range(2):
            part_copy(group, side).start()

    same = lax.rem(me_a + core_at, 2) == 0

    @pl.loop(0, n_turns)
    def _(step):
        odd = lax.rem(step, 2)
        even_far = jnp.where(odd == 1, step + 1, n_angle - step)
        odd_far = jnp.where(odd == 1, n_angle - step, step + 1)
        a = lax.rem(me_a + jnp.where(same, even_far, odd_far), n_angle)
        g = a // 2
        for side in range(2):
            for kind in range(2):
                sender = phase_sender(side, kind)
                dst = ph_all.at[g, side, kind]

                @pl.when(jnp.logical_or(a != me_a, sender != me_s))
                def _():
                    remote(
                        dst, dst, a2a_s.at[kind, 0], a2a_r.at[g, side, kind], strip=mate
                    ).wait_recv()

        rows = jnp.concatenate(
            [ph_all[g, side, 0].astype(F32) + ph_all[g, side, 1].astype(F32) for side in range(2)],
            axis=0,
        ).astype(BF16)
        mirrored = [
            jnp.dot(rows[:, b : b + LANES], flip, preferred_element_type=F32)
            for b in range(0, n_cols, LANES)
        ]
        both = jnp.concatenate(
            [rows.astype(F32), jnp.concatenate(mirrored[::-1], axis=1)], axis=0
        )
        lhs[:64, :] = both.astype(BF16)
        lhs[64:, :] = pltpu.roll(both, n_cols - 1, 1).astype(BF16)

        @pl.loop(0, n_groups)
        def _(group):
            for pair in range(8):
                project(g, group * 8 + pair)

            @pl.when(step == n_turns - 1)
            def _():
                finish_group(group)

        @pl.when(step == 0)
        def _():
            exchange_probe()

        @pl.when(step == n_turns - 1)
        def _():
            finish_object()

        @pl.when(step == 1)
        def _():
            gather_probe()

    @pl.loop(0, n_angle)
    def _(peer):
        for kind in range(2):
            copy, stays, _, _ = phase_copy(kind, peer)

            @pl.when(jnp.logical_not(stays))
            def _():
                copy.wait_send()

    @pl.loop(0, n_groups)
    def _(group):
        for side in range(2):
            part_copy(group, side).wait_recv()
            cols = group_at(group, side)
            vol[core_at, :, cols] += vol_in[:, cols]
            store_part(group, side).start()

    def ag_arrived(d):
        sender = lax.rem(me_s + n_strip - d, n_strip)
        rows = pl.ds(pl.multiple_of(sender * 16, 16), 16)
        return remote(ag_in.at[rows], ag_in.at[rows], ag_s.at[d], ag_r.at[d], strip=sender)

    @pl.loop(1, n_strip)
    def _(d):
        ag_copy(d).wait_send()
        ag_arrived(d).wait_recv()

    pg_out[...] = ag_in[...].astype(F32)
    store_pg = pltpu.make_async_copy(pg_out, pg_hbm, store_sem.at[2])
    store_pg.start()
    @pl.loop(0, n_groups)
    def _(group):
        for side in range(2):
            part_copy(group, side).wait_send()
            store_part(group, side).wait()

    store_og.wait()
    store_pg.wait()


def shards(object_field, amplitudes, scan_offsets, probe_field, tilt_angles):
    n_angle, n_strip = lax.axis_size("angle"), lax.axis_size("strip")
    width = object_field.shape[3]
    fwd, inv = dft_blocks()
    trig = jnp.stack([jnp.cos(tilt_angles), jnp.sin(tilt_angles)])
    scale = 1.0 / math.sqrt(n_angle * n_strip * scan_offsets.shape[1])
    n_cols = WINDOW[1] - WINDOW[0]
    parts = (NG // 32, 2)
    hbm = pl.BlockSpec(memory_space=pltpu.HBM)
    smem = pl.BlockSpec(memory_space=pltpu.SMEM)
    vmem, dma = pltpu.VMEM, pltpu.SemaphoreType.DMA
    object_grad, probe_grad, volume = pl.pallas_call(
        lambda *refs: kernel(n_angle, n_strip, scale, *refs),
        out_shape=(
            jax.ShapeDtypeStruct((2, 128, width), F32),
            jax.ShapeDtypeStruct((2 * FRAME, FRAME), F32),
            jax.ShapeDtypeStruct((16, NG * NG), F32),
        ),
        in_specs=[smem, smem] + [hbm] * 5,
        out_specs=(hbm, hbm, hbm),
        scratch_shapes=[
            vmem((2, FRAME, width), F32),
            vmem((2, FRAME, FRAME), F32),
            vmem((4, FRAME, FRAME), BF16),
            vmem((2 * FRAME, 2 * FRAME), BF16),
            vmem((2 * FRAME, 2 * FRAME), BF16),
            vmem((2, 2, HALO, width), BF16),
            vmem((2, 2, HALO, width), BF16),
            vmem((width, FRAME), BF16),
            vmem((FRAME, width), BF16),
            vmem((2, HALO, width), F32),
            vmem((2, FRAME, FRAME), F32),
            vmem((4, 4 * HALO, 2 * FRAME), BF16),
            vmem((4, 2 * FRAME, FRAME), BF16),
            vmem((4, 2 * FRAME, FRAME), F32),
            vmem((4, 2 * FRAME, FRAME), BF16),
            vmem((4, 4 * HALO, 2 * FRAME), BF16),
            vmem((4 * HALO, 2 * FRAME), F32),
            vmem((2, 2, HALO, width), BF16),
            vmem((2, 2, HALO, width), BF16),
            vmem((2, 128, width), F32),
            vmem((FRAME, n_cols), BF16),
            vmem((n_angle // 2, 2, 2, 16, n_cols), BF16),
            vmem((2 * FRAME, FRAME), BF16),
            vmem((n_strip, 16, FRAME), BF16),
            vmem((n_angle, 16, FRAME), BF16),
            vmem((2 * FRAME, FRAME), BF16),
            vmem((2 * FRAME, FRAME), F32),
            vmem((n_angle // 2, NG // 2, LANES), F32),
            vmem((n_angle // 2, NG // 2, LANES), F32),
            vmem((128, n_cols), BF16),
            vmem((NG // 2, 64, LANES), F32),
            vmem((2, 16, NG * NG), F32),
            vmem((16, NG * NG), F32),
            dma((5,)), dma((3,)), dma((2,)), dma((2,)), dma((2,)), dma((2,)),
            dma((2, n_angle)), dma((n_angle // 2, 2, 2)), dma((n_strip,)), dma((n_strip,)),
            dma((n_angle,)), dma((n_angle,)), dma((n_strip,)), dma((n_strip,)),
            dma(parts), dma(parts), dma(parts),
        ],
        compiler_params=pltpu.CompilerParams(
            collective_id=0, has_side_effects=True, vmem_limit_bytes=60 * 1024 * 1024
        ),
        name="gradient_step",
    )(
        scan_offsets.transpose(0, 2, 1), trig, object_field[:, 0], amplitudes[0], probe_field, fwd, inv
    )
    return (
        object_grad[:, None],
        probe_grad.reshape(2, FRAME, FRAME),
        volume[None, None],
    )


def solution(mesh):
    return jax.shard_map(
        shards,
        mesh=mesh,
        in_specs=(
            P(None, "angle", "strip", None),
            P("angle", "strip", None, None),
            P("angle", "strip", None),
            P(),
            P(),
        ),
        out_specs=(P(None, "angle", "strip", None), P(), P("strip", "angle", None, None)),
        check_vma=False,
    )
```

```python
import math

import jax
import jax.numpy as jnp
import numpy as np
from jax import lax
from jax.experimental import pallas as pl
from jax.experimental.pallas import tpu as pltpu
from jax.sharding import PartitionSpec as P

FRAME = 256
HALO = 64
NG = 128
LANES = 128
MESH = pl.DeviceIdType.MESH
F32 = jnp.float32
BF16 = jnp.bfloat16
FIXED_COLS = (768, 0, 384)
WINDOW = (320, 704)


def dft_blocks():
    index = np.arange(FRAME)
    angle = 2.0 * np.pi / FRAME * ((index[:, None] * index[None, :]) % FRAME)
    cos_tab = np.cos(angle) / math.sqrt(FRAME)
    sin_tab = np.sin(angle) / math.sqrt(FRAME)
    fwd = np.block([[cos_tab, sin_tab], [-sin_tab, cos_tab]])
    inv = np.block([[cos_tab, -sin_tab], [sin_tab, cos_tab]])
    return jnp.asarray(fwd, BF16), jnp.asarray(inv, BF16)


def kernel(
    n_angle, n_strip, scale,
    offs, trig, obj_hbm, amp_hbm, probe_hbm, fwd_hbm, inv_hbm,
    og_hbm, pg_hbm, vol_hbm,
    ext, probe, amp, fwd, inv,
    halo_out, halo_in, place_t, place_m, moved3, patch3, xbuf, ybuf, wbuf, mbuf, zbuf, gbuf,
    grad_out, grad_in, core, phase, ph_all,
    pterm, rs_in, ar_in, ag_in, pg_out,
    lower_t, frac_t, lhs, total, vol, vol_in,
    load_sem, store_sem, halo_s, halo_r, grad_s, grad_r, a2a_s, a2a_r,
    rs_s, rs_r, ar_s, ar_r, ag_s, ag_r, part_s, part_r, own_sem,
):
    width = ext.shape[2]
    me_a = lax.axis_index("angle")
    me_s = lax.axis_index("strip")
    above = lax.rem(me_s + n_strip - 1, n_strip)
    below = lax.rem(me_s + 1, n_strip)
    core_at = lax.rem(me_s, 2)
    mate = me_s + 1 - 2 * core_at

    loads = [
        pltpu.make_async_copy(obj_hbm, ext.at[:, pl.ds(HALO, 128), :], load_sem.at[0]),
        pltpu.make_async_copy(probe_hbm, probe, load_sem.at[1]),
        pltpu.make_async_copy(inv_hbm, inv, load_sem.at[2]),
        pltpu.make_async_copy(fwd_hbm, fwd, load_sem.at[3]),
        pltpu.make_async_copy(amp_hbm, amp, load_sem.at[4]),
    ]
    for load in loads:
        load.start()

    barrier = pltpu.get_barrier_semaphore()

    pl.semaphore_signal(barrier, inc=1, device_id={"strip": above}, device_id_type=MESH)

    @pl.loop(1, n_strip - 1)
    def _(d):
        pl.semaphore_signal(
            barrier, inc=1, device_id={"strip": lax.rem(me_s + d, n_strip)}, device_id_type=MESH
        )

    @pl.loop(1, n_angle)
    def _(d):
        pl.semaphore_signal(
            barrier, inc=1, device_id={"angle": lax.rem(me_a + d, n_angle)}, device_id_type=MESH
        )

    def phase_sender(side, kind):
        strip_to = me_s - core_at + side
        if kind == 0:
            return strip_to
        neighbour = jnp.where(me_a >= n_angle // 2, strip_to + 1, strip_to + n_strip - 1)
        return lax.rem(neighbour, n_strip)

    def phase_target(kind, peer):
        if kind == 0:
            row, strip_to = HALO + peer * 16, me_s
        else:
            upper = peer >= n_angle // 2
            row = jnp.where(upper, (peer - n_angle // 2) * 16, 3 * HALO + peer * 16)
            strip_to = jnp.where(upper, above, below)
        side = lax.rem(strip_to, 2)
        return row, side, strip_to - side + lax.rem(me_a, 2)

    @pl.loop(0, n_angle // 2)
    def _(g):
        a = 2 * g + core_at
        for side in range(2):
            for kind in range(2):
                sender = phase_sender(side, kind)

                @pl.when(jnp.logical_or(a != me_a, sender != me_s))
                def _():
                    pl.semaphore_signal(
                        barrier, inc=1, device_id={"angle": a, "strip": sender}, device_id_type=MESH
                    )

    messages = 2 * n_angle
    for kind in range(2):
        messages = messages - jnp.where(phase_target(kind, me_a)[2] == me_s, 1, 0)

    loads[0].wait()
    for side, first in ((0, HALO), (1, 2 * HALO)):

        @pl.loop(0, 4)
        def _(step):
            rows = pl.multiple_of(step * 16, 16)
            for part in range(2):
                halo_out[side, part, pl.ds(rows, 16), :] = ext[
                    part, pl.ds(first + rows, 16), :
                ].astype(BF16)

    pl.semaphore_wait(barrier, n_strip - 1 + n_angle - 1 + messages)

    def remote(src, dst, send, recv, **where):
        return pltpu.make_async_remote_copy(
            src_ref=src, dst_ref=dst, send_sem=send, recv_sem=recv,
            device_id=where, device_id_type=MESH,
        )

    halo_copies = [
        remote(halo_out.at[1], halo_in.at[0], halo_s.at[0], halo_r.at[0], strip=below),
        remote(halo_out.at[0], halo_in.at[1], halo_s.at[1], halo_r.at[1], strip=above),
    ]
    for copy in halo_copies:
        copy.start()

    col = offs[0, 1, 3].astype(F32)
    for b in range(width // LANES):
        at = lax.broadcasted_iota(jnp.int32, (LANES, FRAME), 0) + b * LANES
        of = lax.broadcasted_iota(jnp.int32, (LANES, FRAME), 1)
        place_t[b * LANES : (b + 1) * LANES, :] = ((at - of).astype(F32) == col).astype(F32).astype(BF16)
        at = lax.broadcasted_iota(jnp.int32, (FRAME, LANES), 1) + b * LANES
        of = lax.broadcasted_iota(jnp.int32, (FRAME, LANES), 0)
        place_m[:, b * LANES : (b + 1) * LANES] = ((at - of).astype(F32) == col).astype(F32).astype(BF16)

    def split(value):
        high = value.astype(BF16)
        return jnp.concatenate([high, (value - high.astype(F32)).astype(BF16)], axis=0)

    def joined(product):
        rows = product.shape[0] // 2
        return product[:rows] + product[rows:]

    def exit_chunk(chunk):
        rows = pl.ds(chunk * HALO, HALO)
        for part in range(2):
            patch3[part, rows, :] = joined(
                jnp.dot(split(ext[part, rows, :]), place_t[...], preferred_element_type=F32)
            )

        @pl.loop(0, 4)
        def _(step):
            local = pl.multiple_of(step * 16, 16)
            row = chunk * HALO + local
            pr, pi = probe[0, pl.ds(row, 16), :], probe[1, pl.ds(row, 16), :]
            res, ims = [
                [ext[part, pl.ds(row, 16), c : c + FRAME] for c in FIXED_COLS]
                + [patch3[part, pl.ds(row, 16), :]]
                for part in range(2)
            ]
            for f in range(4):
                xbuf[chunk, pl.ds(f * HALO + local, 16), :FRAME] = (
                    pr * res[f] - pi * ims[f]
                ).astype(BF16)
                xbuf[chunk, pl.ds(f * HALO + local, 16), FRAME:] = (
                    pr * ims[f] + pi * res[f]
                ).astype(BF16)

        half = jnp.dot(xbuf[chunk], inv[...], preferred_element_type=F32).astype(BF16)
        for f in range(4):
            at = f * HALO
            ybuf[f, pl.ds(chunk * HALO, HALO), :] = half[at : at + HALO, :FRAME]
            ybuf[f, pl.ds(FRAME + chunk * HALO, HALO), :] = half[at : at + HALO, FRAME:]

    loads[1].wait()
    loads[2].wait()
    exit_chunk(1)
    exit_chunk(2)

    center = (NG - 1) / 2.0
    n_rows = NG // 2
    shape = (n_rows, LANES)
    xpos = lax.broadcasted_iota(jnp.int32, shape, 0).astype(F32) - center
    ypos = lax.broadcasted_iota(jnp.int32, shape, 1).astype(F32) - center
    n_turns = n_angle // 2

    @pl.loop(0, n_turns)
    def _(g):
        a = 2 * g + core_at
        upos = (width - 1) / 2.0 + 2.0 * (xpos * trig[0, a] + ypos * trig[1, a])
        low = jnp.clip(jnp.floor(upos), 0.0, width - 2.0)
        lower_t[g] = low - float(WINDOW[0])
        frac_t[g] = upos - low
        each = n_rows // n_turns
        total[pl.ds(g * each, each)] = jnp.zeros((each, 64, LANES), F32)

    for copy in halo_copies:
        copy.wait()
    has_above = (me_s > 0).astype(F32)
    has_below = (me_s < n_strip - 1).astype(F32)
    for side, first, present in ((0, 0, has_above), (1, 3 * HALO, has_below)):

        @pl.loop(0, 4)
        def _(step):
            rows = pl.multiple_of(step * 16, 16)
            for part in range(2):
                ext[part, pl.ds(first + rows, 16), :] = (
                    halo_in[side, part, pl.ds(rows, 16), :].astype(F32) * present
                )

    exit_chunk(0)
    exit_chunk(3)

    loads[3].wait()
    loads[4].wait()

    def misfit(f, rows):
        wr, wi = wbuf[f, rows, :], wbuf[f, rows.start + FRAME : rows.stop + FRAME, :]
        measured = amp[f, rows, :].astype(F32)
        factor = 1.0 - measured * lax.rsqrt(wr * wr + wi * wi + 1.0)
        mbuf[f, rows, :] = (wr * factor).astype(BF16)
        mbuf[f, rows.start + FRAME : rows.stop + FRAME, :] = (wi * factor).astype(BF16)

    for f in range(4):
        wbuf[f] = jnp.dot(fwd[...], ybuf[f], preferred_element_type=F32)
        for row in range(0, FRAME, 32):
            misfit(f, slice(row, row + 32))
    for f in range(4):
        back = jnp.dot(inv[...], mbuf[f], preferred_element_type=F32).astype(BF16)
        for chunk in range(4):
            at = chunk * HALO
            zbuf[chunk, f * HALO : (f + 1) * HALO, :FRAME] = back[at : at + HALO]
            zbuf[chunk, f * HALO : (f + 1) * HALO, FRAME:] = back[FRAME + at : FRAME + at + HALO]

    def place(terms, moved):
        blocks = [moved[:, b * LANES : (b + 1) * LANES] for b in range(width // LANES)]
        for f in range(3):
            b = FIXED_COLS[f] // LANES
            blocks[b] = blocks[b] + terms[f][:, :LANES]
            blocks[b + 1] = blocks[b + 1] + terms[f][:, LANES:]
        return blocks

    around = (WINDOW[0] // LANES * LANES, -(-WINDOW[1] // LANES) * LANES)

    def grad_chunk(chunk):
        gbuf[...] = jnp.dot(zbuf[chunk], fwd[...], preferred_element_type=F32)
        rows = pl.ds(chunk * HALO, HALO)
        pr, pi = probe[0, rows, :], probe[1, rows, :]
        gr, gi = gbuf[3 * HALO :, :FRAME], gbuf[3 * HALO :, FRAME:]
        for part, value in ((0, pr * gr + pi * gi), (1, pr * gi - pi * gr)):
            moved3[part] = joined(
                jnp.dot(split(value), place_m[...], preferred_element_type=F32)
            )

        @pl.loop(0, 4)
        def _(step):
            local = pl.multiple_of(step * 16, 16)
            row = chunk * HALO + local
            rows = pl.ds(row, 16)
            pr, pi = probe[0, rows, :], probe[1, rows, :]
            t_re, t_im, q_re, q_im = [], [], 0.0, 0.0
            for f in range(4):
                gr = gbuf[pl.ds(f * HALO + local, 16), :FRAME]
                gi = gbuf[pl.ds(f * HALO + local, 16), FRAME:]
                if f < 3:
                    t_re.append(pr * gr + pi * gi)
                    t_im.append(pr * gi - pi * gr)
                    c = FIXED_COLS[f]
                    er, ei = ext[0, rows, c : c + FRAME], ext[1, rows, c : c + FRAME]
                else:
                    er, ei = patch3[0, rows, :], patch3[1, rows, :]
                q_re = q_re + (er * gr + ei * gi)
                q_im = q_im + (er * gi - ei * gr)
            pterm[pl.ds(row, 16), :] = q_re.astype(BF16)
            pterm[pl.ds(FRAME + row, 16), :] = q_im.astype(BF16)
            sums = [
                place(terms, moved3[part, pl.ds(local, 16), :])
                for part, terms in ((0, t_re), (1, t_im))
            ]
            for part in range(2):
                for b, value in enumerate(sums[part]):
                    cols = slice(b * LANES, (b + 1) * LANES)
                    if chunk in (0, 3):
                        grad_out[chunk // 3, part, pl.ds(local, 16), cols] = value.astype(BF16)
                    else:
                        core[part, pl.ds((chunk - 1) * HALO + local, 16), cols] = value
            value = jnp.concatenate(
                [
                    ext[0, rows, b * LANES : (b + 1) * LANES] * sums[1][b]
                    - ext[1, rows, b * LANES : (b + 1) * LANES] * sums[0][b]
                    for b in range(around[0] // LANES, around[1] // LANES)
                ],
                axis=1,
            )
            value = pltpu.roll(value, around[1] - WINDOW[0], 1)
            phase[rows, :] = value[:, : WINDOW[1] - WINDOW[0]].astype(BF16)

    def phase_copy(kind, peer):
        row, side, to = phase_target(kind, peer)
        src = phase.at[pl.ds(pl.multiple_of(row, 16), 16)]
        dst = ph_all.at[me_a // 2, side, kind]
        copy = remote(
            src, dst, a2a_s.at[kind, peer], a2a_r.at[me_a // 2, side, kind], angle=peer, strip=to
        )
        stays = jnp.logical_and(peer == me_a, to == me_s)
        return copy, stays, src, dst

    def send_phase(kind, first):
        @pl.loop(first, first + n_angle // 2)
        def _(peer):
            copy, stays, src, dst = phase_copy(kind, peer)

            @pl.when(stays)
            def _():
                dst[...] = src[...]

            @pl.when(jnp.logical_not(stays))
            def _():
                copy.start()

    grad_chunk(0)
    send_phase(1, n_angle // 2)
    grad_chunk(3)
    send_phase(1, 0)
    grad_chunk(1)
    send_phase(0, 0)
    grad_chunk(2)
    send_phase(0, n_angle // 2)

    def rs_copy(d):
        peer = lax.rem(me_s + d, n_strip)
        return remote(
            pterm.at[pl.ds(pl.multiple_of(peer * 16, 16), 16)], rs_in.at[d],
            rs_s.at[d], rs_r.at[d], strip=peer,
        )

    @pl.loop(1, n_strip)
    def _(d):
        rs_copy(d).start()

    grad_copies = [
        remote(grad_out.at[1], grad_in.at[0], grad_s.at[0], grad_r.at[0], strip=below),
        remote(grad_out.at[0], grad_in.at[1], grad_s.at[1], grad_r.at[1], strip=above),
    ]
    for copy in grad_copies:
        copy.start()

    own_rows = pl.ds(pl.multiple_of(me_s * 16, 16), 16)

    def ar_copy(d):
        peer = lax.rem(me_a + d, n_angle)
        return remote(
            ar_in.at[me_a], ar_in.at[me_a], ar_s.at[d], ar_r.at[d], angle=peer
        )

    store_og = pltpu.make_async_copy(core, og_hbm, store_sem.at[0])

    def finish_object():
        for copy in grad_copies:
            copy.wait()
        for side, present in ((0, has_above), (1, has_below)):

            @pl.loop(0, 4)
            def _(step):
                local = pl.multiple_of(step * 16, 16)
                rows = pl.ds(side * HALO + local, 16)
                for part in range(2):
                    core[part, rows, :] += (
                        grad_in[side, part, pl.ds(local, 16), :].astype(F32) * present
                    )

        store_og.start()

    def exchange_probe():
        @pl.loop(1, n_strip)
        def _(d):
            rs_copy(d).wait()

        ar_in[me_a] = lax.fori_loop(
            1, n_strip, lambda d, acc: acc + rs_in[d].astype(F32), pterm[own_rows, :].astype(F32)
        ).astype(BF16)

        @pl.loop(1, n_angle)
        def _(d):
            ar_copy(d).start()

    flip = (
        lax.broadcasted_iota(jnp.int32, (LANES, LANES), 0)
        + lax.broadcasted_iota(jnp.int32, (LANES, LANES), 1)
        == LANES - 1
    ).astype(F32).astype(BF16)
    n_cols = WINDOW[1] - WINDOW[0]
    column = lax.broadcasted_iota(jnp.int32, (LANES, LANES), 0).astype(F32).astype(BF16)
    one, zero = jnp.ones((), BF16), jnp.zeros((), BF16)

    def ag_copy(d):
        peer = lax.rem(me_s + d, n_strip)
        return remote(
            ag_in.at[own_rows], ag_in.at[own_rows], ag_s.at[d], ag_r.at[d], strip=peer
        )

    def gather_probe():
        @pl.loop(1, n_angle)
        def _(d):
            ar_copy(d).wait()

        summed = ar_in[0].astype(F32)
        for a in range(1, n_angle):
            summed = summed + ar_in[a].astype(F32)
        ag_in[own_rows, :] = (summed * scale).astype(BF16)

        @pl.loop(1, n_strip)
        def _(d):
            ag_copy(d).start()

    def one_hot(g, i):
        low = lower_t[g, pl.ds(i, 1), :]
        return jnp.concatenate(
            [
                jnp.where(column == (low - float(j)).astype(BF16), one, zero)
                for j in range(0, n_cols, LANES)
            ],
            axis=0,
        )

    def project(g, pair):
        picks = jnp.concatenate([one_hot(g, 2 * pair + k) for k in range(2)], axis=1)
        got = jnp.dot(lhs[...], picks, preferred_element_type=F32)
        for k in range(2):
            frac = frac_t[g, pl.ds(2 * pair + k, 1), :]
            part = got[:, k * LANES : (k + 1) * LANES]
            total[2 * pair + k] += part[:64] * (1.0 - frac) + part[64:] * frac

    n_groups = n_rows // 16
    group_cols = 16 * LANES

    def group_at(group, side):
        row = group * 16
        if side:
            row = NG - row - 16
        return pl.ds(pl.multiple_of(row * LANES, LANES), group_cols)

    def part_copy(group, side):
        cols = group_at(group, side)
        return remote(
            vol.at[1 - core_at, :, cols], vol_in.at[:, cols],
            part_s.at[group, side], part_r.at[group, side], strip=mate,
        )

    def store_part(group, side):
        cols = group_at(group, side)
        return pltpu.make_async_copy(
            vol.at[core_at, :, cols], vol_hbm.at[:, cols], own_sem.at[group, side]
        )

    def finish_group(group):
        stack = jnp.concatenate([total[group * 16 + k, 32:] for k in range(16)], axis=0)
        turned = joined(jnp.dot(split(stack), flip, preferred_element_type=F32))
        for k in range(16):
            x = group * 16 + k
            here = pl.ds(pl.multiple_of(x * LANES, LANES), LANES)
            there = pl.ds(pl.multiple_of((NG - 1 - x) * LANES, LANES), LANES)
            for c in range(2):
                vol[c, :, here] = total[x, c * 16 : c * 16 + 16]
                vol[c, :, there] = turned[k * 32 + c * 16 : k * 32 + c * 16 + 16]
        for side in range(2):
            part_copy(group, side).start()

    same = lax.rem(me_a + core_at, 2) == 0

    @pl.loop(0, n_turns)
    def _(step):
        odd = lax.rem(step, 2)
        even_far = jnp.where(odd == 1, step + 1, n_angle - step)
        odd_far = jnp.where(odd == 1, n_angle - step, step + 1)
        a = lax.rem(me_a + jnp.where(same, even_far, odd_far), n_angle)
        g = a // 2
        for side in range(2):
            for kind in range(2):
                sender = phase_sender(side, kind)
                dst = ph_all.at[g, side, kind]

                @pl.when(jnp.logical_or(a != me_a, sender != me_s))
                def _():
                    remote(
                        dst, dst, a2a_s.at[kind, 0], a2a_r.at[g, side, kind], strip=mate
                    ).wait_recv()

        rows = jnp.concatenate(
            [ph_all[g, side, 0].astype(F32) + ph_all[g, side, 1].astype(F32) for side in range(2)],
            axis=0,
        ).astype(BF16)
        mirrored = [
            jnp.dot(rows[:, b : b + LANES], flip, preferred_element_type=F32)
            for b in range(0, n_cols, LANES)
        ]
        both = jnp.concatenate(
            [rows.astype(F32), jnp.concatenate(mirrored[::-1], axis=1)], axis=0
        )
        lhs[:64, :] = both.astype(BF16)
        lhs[64:, :] = pltpu.roll(both, n_cols - 1, 1).astype(BF16)

        @pl.loop(0, n_groups)
        def _(group):
            for pair in range(8):
                project(g, group * 8 + pair)

            @pl.when(step == n_turns - 1)
            def _():
                finish_group(group)

        @pl.when(step == 0)
        def _():
            exchange_probe()

        @pl.when(step == n_turns - 1)
        def _():
            finish_object()

        @pl.when(step == 1)
        def _():
            gather_probe()

    @pl.loop(0, n_angle)
    def _(peer):
        for kind in range(2):
            copy, stays, _, _ = phase_copy(kind, peer)

            @pl.when(jnp.logical_not(stays))
            def _():
                copy.wait_send()

    @pl.loop(0, n_groups)
    def _(group):
        for side in range(2):
            part_copy(group, side).wait_recv()
            cols = group_at(group, side)
            vol[core_at, :, cols] += vol_in[:, cols]
            store_part(group, side).start()

    def ag_arrived(d):
        sender = lax.rem(me_s + n_strip - d, n_strip)
        rows = pl.ds(pl.multiple_of(sender * 16, 16), 16)
        return remote(ag_in.at[rows], ag_in.at[rows], ag_s.at[d], ag_r.at[d], strip=sender)

    @pl.loop(1, n_strip)
    def _(d):
        ag_copy(d).wait_send()
        ag_arrived(d).wait_recv()

    pg_out[...] = ag_in[...].astype(F32)
    store_pg = pltpu.make_async_copy(pg_out, pg_hbm, store_sem.at[2])
    store_pg.start()
    @pl.loop(0, n_groups)
    def _(group):
        for side in range(2):
            part_copy(group, side).wait_send()
            store_part(group, side).wait()

    store_og.wait()
    store_pg.wait()


def deliver(object_in, probe_in, volume_in, object_out, probe_out, volume_out,
            object_buf, probe_buf, volume_buf, in_sem, out_sem):
    loads, stores = [], []
    for part in range(4):
        half = (part // 2, pl.ds(part % 2 * 64, 64))
        rows = pl.ds(part * 128, 128)
        cols = (slice(None), pl.ds(part * 4096, 4096))
        for i, (src, buf, dst, at) in enumerate(
            (
                (object_in, object_buf, object_out, half),
                (volume_in, volume_buf, volume_out, cols),
                (probe_in, probe_buf, probe_out, rows),
            )
        ):
            loads.append(pltpu.make_async_copy(src.at[at], buf.at[at], in_sem.at[i, part]))
            stores.append(pltpu.make_async_copy(buf.at[at], dst.at[at], out_sem.at[i, part]))
    for load in loads:
        load.start()
    for load, store in zip(loads, stores):
        load.wait()
        store.start()
    for store in stores:
        store.wait()


def shards(object_field, amplitudes, scan_offsets, probe_field, tilt_angles):
    n_angle, n_strip = lax.axis_size("angle"), lax.axis_size("strip")
    width = object_field.shape[3]
    fwd, inv = dft_blocks()
    trig = jnp.stack([jnp.cos(tilt_angles), jnp.sin(tilt_angles)])
    scale = 1.0 / math.sqrt(n_angle * n_strip * scan_offsets.shape[1])
    n_cols = WINDOW[1] - WINDOW[0]
    parts = (NG // 32, 2)
    hbm = pl.BlockSpec(memory_space=pltpu.HBM)
    smem = pl.BlockSpec(memory_space=pltpu.SMEM)
    vmem, dma = pltpu.VMEM, pltpu.SemaphoreType.DMA
    object_grad, probe_grad, volume = pl.pallas_call(
        lambda *refs: kernel(n_angle, n_strip, scale, *refs),
        out_shape=(
            jax.ShapeDtypeStruct((2, 128, width), F32),
            jax.ShapeDtypeStruct((2 * FRAME, FRAME), F32),
            jax.ShapeDtypeStruct((16, NG * NG), F32),
        ),
        in_specs=[smem, smem] + [hbm] * 5,
        out_specs=(hbm, hbm, hbm),
        scratch_shapes=[
            vmem((2, FRAME, width), F32),
            vmem((2, FRAME, FRAME), F32),
            vmem((4, FRAME, FRAME), BF16),
            vmem((2 * FRAME, 2 * FRAME), BF16),
            vmem((2 * FRAME, 2 * FRAME), BF16),
            vmem((2, 2, HALO, width), BF16),
            vmem((2, 2, HALO, width), BF16),
            vmem((width, FRAME), BF16),
            vmem((FRAME, width), BF16),
            vmem((2, HALO, width), F32),
            vmem((2, FRAME, FRAME), F32),
            vmem((4, 4 * HALO, 2 * FRAME), BF16),
            vmem((4, 2 * FRAME, FRAME), BF16),
            vmem((4, 2 * FRAME, FRAME), F32),
            vmem((4, 2 * FRAME, FRAME), BF16),
            vmem((4, 4 * HALO, 2 * FRAME), BF16),
            vmem((4 * HALO, 2 * FRAME), F32),
            vmem((2, 2, HALO, width), BF16),
            vmem((2, 2, HALO, width), BF16),
            vmem((2, 128, width), F32),
            vmem((FRAME, n_cols), BF16),
            vmem((n_angle // 2, 2, 2, 16, n_cols), BF16),
            vmem((2 * FRAME, FRAME), BF16),
            vmem((n_strip, 16, FRAME), BF16),
            vmem((n_angle, 16, FRAME), BF16),
            vmem((2 * FRAME, FRAME), BF16),
            vmem((2 * FRAME, FRAME), F32),
            vmem((n_angle // 2, NG // 2, LANES), F32),
            vmem((n_angle // 2, NG // 2, LANES), F32),
            vmem((128, n_cols), BF16),
            vmem((NG // 2, 64, LANES), F32),
            vmem((2, 16, NG * NG), F32),
            vmem((16, NG * NG), F32),
            dma((5,)), dma((3,)), dma((2,)), dma((2,)), dma((2,)), dma((2,)),
            dma((2, n_angle)), dma((n_angle // 2, 2, 2)), dma((n_strip,)), dma((n_strip,)),
            dma((n_angle,)), dma((n_angle,)), dma((n_strip,)), dma((n_strip,)),
            dma(parts), dma(parts), dma(parts),
        ],
        compiler_params=pltpu.CompilerParams(
            collective_id=0, has_side_effects=True, vmem_limit_bytes=60 * 1024 * 1024
        ),
        name="gradient_step",
    )(
        scan_offsets.transpose(0, 2, 1), trig, object_field[:, 0], amplitudes[0], probe_field, fwd, inv
    )
    results = (object_grad, probe_grad, volume)
    object_grad, probe_grad, volume = pl.pallas_call(
        deliver,
        out_shape=tuple(jax.ShapeDtypeStruct(r.shape, r.dtype) for r in results),
        in_specs=[hbm] * 3,
        out_specs=(hbm,) * 3,
        scratch_shapes=[vmem(r.shape, r.dtype) for r in results] + [dma((3, 4)), dma((3, 4))],
        compiler_params=pltpu.CompilerParams(vmem_limit_bytes=60 * 1024 * 1024),
        name="deliver",
    )(*results)
    return (
        object_grad[:, None],
        probe_grad.reshape(2, FRAME, FRAME),
        volume[None, None],
    )


def solution(mesh):
    return jax.shard_map(
        shards,
        mesh=mesh,
        in_specs=(
            P(None, "angle", "strip", None),
            P("angle", "strip", None, None),
            P("angle", "strip", None),
            P(),
            P(),
        ),
        out_specs=(P(None, "angle", "strip", None), P(), P("strip", "angle", None, None)),
        check_vma=False,
    )
```
